256 devices in a mesh: img: 8 (over x, z_hi), tile: 32 (over z_lo, y, core).
Axes of the slice: x: 4, y: 4, z: 8 (z_hi: 2, z_lo: 4; z = z_hi * 4 + z_lo), core: 2. Of those that a mesh axis runs over, the one named last changes fastest.
Arguments:
- block_feature_map: bfloat16 [8, 192, 256, 256], P('img', None, 'tile'), may hold values from -12 to 12, as said below
- upstream_sensitivity: bfloat16 [8, 192, 256, 256], P('img', None, 'tile'), may hold values from -12 to 12, as said below
- triple_mixer: bfloat16 [576, 192], replicated, may hold values from -0.4375 to 0.4375
- spatial_stencil: float32 [576, 3, 3], replicated, may hold values from -2 to 2
- outgoing_mixer: bfloat16 [192, 192], replicated, may hold values from -0.4375 to 0.4375
- sharpness_factor: float32 [4], replicated, may hold values from 1 to 8
- standardize_scaling: float32 [192], replicated, may hold values from 0.5 to 1.5
- standardize_offset: float32 [192], replicated, may hold values from -1.5 to 1.5
Outputs:
- feature_map_adjoint: bfloat16 [8, 192, 256, 256], P('img', None, 'tile')
- triple_mixer_adjoint: float32 [576, 192], replicated
- spatial_stencil_adjoint: float32 [576, 3, 3], replicated
- outgoing_mixer_adjoint: float32 [192, 192], replicated
- sharpness_adjoint: float32 [4], replicated
- scaling_adjoint: float32 [192], replicated
- offset_adjoint: float32 [192], replicated
The draws below stay inside these ranges and needn't reach their ends.
Inputs may be any that keep to these rules, and one draw needn't show every extreme that they name: `block_feature_map`: the block's input feature map. `upstream_sensitivity`: gradient of the loss with respect to the block's output.
All inputs are finite; a program needn't handle non-finite values.
Results may differ from the reference program's by a relative error of at most 0.0072.
Values may be sent and summed in bfloat16 or wider, within the bound.
No kernel may reach another device: no remote copies, remote signals or barrier semaphores. Data moves between devices by JAX's collectives and lax.ppermute only.
A program may use at most 64 MiB of HBM per device.

```python
import math
import jax
import jax.numpy as jnp
from jax import lax

C = 192
ATTN_GROUP_COUNT = 4
W = 256
H = 256
B = 8


def draw_block_feature_map(key, part):
    key_noise, key_slope = jax.random.split(jax.random.fold_in(key, 7), 2)
    row_place = 2.0 * jnp.arange(H, dtype=jnp.float32) / max(H - 1, 1) - 1.0
    slope = jax.random.uniform(key_slope, (C,), jnp.float32, -1.0, 1.0)
    channel_scale = jnp.exp(slope[:, None] * row_place[None, :] * math.log(3.0))
    noise = jnp.clip(jax.random.normal(key_noise, (B, C, H, W), jnp.float32), -4.0, 4.0)
    values = noise * channel_scale[None, :, :, None]
    return jnp.clip(values, -12.0, 12.0).astype(jnp.bfloat16)


def draw_upstream_sensitivity(key, part):
    key_noise, key_rows = jax.random.split(key, 2)
    row_place = jnp.arange(H, dtype=jnp.float32) / max(H - 1, 1)
    roughness = jax.random.uniform(key_rows, (H,), jnp.float32, 0.6, 1.4)
    row_scale = jnp.exp(row_place * math.log(3.0)) * roughness
    noise = jnp.clip(jax.random.normal(key_noise, (B, C, H, W), jnp.float32), -4.0, 4.0)
    return jnp.clip(noise * row_scale[None, None, :, None], -12.0, 12.0).astype(jnp.bfloat16)


def normal_values(key, dims, scale, limit, held_as=jnp.bfloat16):
    result = jax.random.normal(key, dims, jnp.float32) * scale
    return jnp.minimum(jnp.maximum(result, -limit), limit).astype(held_as)


def setup_inputs(seed: int = 0) -> dict:
    key_of = jax.random.split(jax.random.key(seed), 9)
    block_feature_map = draw_block_feature_map(jax.random.fold_in(key_of[8], 71), 0)
    upstream_sensitivity = draw_upstream_sensitivity(jax.random.fold_in(key_of[8], 71), 0)
    triple_mixer = normal_values(key_of[2], (3 * C, C), C ** -0.5, 0.4375)
    spatial_stencil = normal_values(key_of[3], (3 * C, 3, 3), 9 ** -0.5, 2.0, jnp.float32)
    outgoing_mixer = normal_values(key_of[4], (C, C), C ** -0.5, 0.4375)
    sharpness_factor = jnp.clip(jnp.exp(jax.random.uniform(key_of[5], (ATTN_GROUP_COUNT,), jnp.float32, math.log(1.0), math.log(8.0))), 1.0, 8.0)
    standardize_scaling = jnp.clip(1.0 + 0.1 * jax.random.normal(key_of[6], (C,), jnp.float32), 0.5, 1.5)
    standardize_offset = normal_values(key_of[7], (C,), 0.3, 1.5, jnp.float32)
    return {"block_feature_map": block_feature_map, "upstream_sensitivity": upstream_sensitivity, "triple_mixer": triple_mixer, "spatial_stencil": spatial_stencil, "outgoing_mixer": outgoing_mixer, "sharpness_factor": sharpness_factor, "standardize_scaling": standardize_scaling, "standardize_offset": standardize_offset}


def depthwise(padded, spatial_stencil):
    row_count = padded.shape[-2] - 2
    col_count = padded.shape[-1]
    widened = jnp.pad(padded.astype(jnp.float32), [(0, 0)] * (padded.ndim - 1) + [(1, 1)])
    summed = jnp.zeros(padded.shape[:-2] + (row_count, col_count), jnp.float32)
    for row_off in range(3):
        for col_off in range(3):
            summed = summed + spatial_stencil[:, row_off, col_off, None, None] * widened[..., row_off:row_off + row_count, col_off:col_off + col_count]
    return summed

def depthwise_back(padded, spatial_stencil):
    row_count = padded.shape[-2] - 2
    col_count = padded.shape[-1]
    widened = jnp.pad(padded.astype(jnp.float32), [(0, 0)] * (padded.ndim - 1) + [(1, 1)])
    summed = jnp.zeros(padded.shape[:-2] + (row_count, col_count), jnp.float32)
    for row_off in range(3):
        for col_off in range(3):
            summed = summed + spatial_stencil[:, row_off, col_off, None, None] * widened[..., 2 - row_off:2 - row_off + row_count, 2 - col_off:2 - col_off + col_count]
    return summed

def kernel_grad(grad_mixed, padded):
    row_count = grad_mixed.shape[-2]
    col_count = grad_mixed.shape[-1]
    grad_float = grad_mixed.astype(jnp.float32)
    widened = jnp.pad(padded.astype(jnp.float32), [(0, 0)] * (padded.ndim - 1) + [(1, 1)])
    reduce_axes = tuple((i for i in range(grad_mixed.ndim) if i != grad_mixed.ndim - 3))
    partials = []
    for row_off in range(3):
        for col_off in range(3):
            partials.append(lax.optimization_barrier(jnp.sum(grad_float * widened[..., row_off:row_off + row_count, col_off:col_off + col_count], axis=reduce_axes)))
    return jnp.stack(partials, axis=-1).reshape(grad_mixed.shape[-3], 3, 3)

def lone_sample(block_feature_map, upstream_sensitivity, triple_mixer, spatial_stencil, outgoing_mixer, sharpness_factor, standardize_scaling, standardize_offset):
    channels, row_count, col_count = block_feature_map.shape
    group_ordinal = sharpness_factor.shape[0]
    head_size = channels // group_ordinal
    pixel_count = row_count * col_count
    as_float = block_feature_map.astype(jnp.float32)
    average = lax.optimization_barrier(jnp.mean(as_float, axis=0, keepdims=True))
    centered = as_float - average
    inverse = lax.rsqrt(lax.optimization_barrier(jnp.mean(centered * centered, axis=0, keepdims=True)) + 1e-05)
    standard = centered * inverse
    normed = (standard * standardize_scaling[:, None, None] + standardize_offset[:, None, None]).astype(jnp.bfloat16)
    projected = jnp.einsum('oc,chw->ohw', triple_mixer.astype(jnp.float32), normed.astype(jnp.float32)).astype(jnp.bfloat16)
    padded = jnp.pad(projected, ((0, 0), (1, 1), (0, 0)))
    mixed = depthwise(padded, spatial_stencil).astype(jnp.bfloat16)
    query_part = mixed[:channels].reshape(group_ordinal, head_size, pixel_count).astype(jnp.float32)
    key_part = mixed[channels:2 * channels].reshape(group_ordinal, head_size, pixel_count).astype(jnp.float32)
    value_part = mixed[2 * channels:].reshape(group_ordinal, head_size, pixel_count).astype(jnp.float32)
    gram_raw = jnp.einsum('hip,hjp->hij', query_part, key_part)
    query_sq = lax.optimization_barrier(jnp.sum(query_part * query_part, axis=2))
    key_sq = lax.optimization_barrier(jnp.sum(key_part * key_part, axis=2))
    query_len = jnp.sqrt(query_sq + 1e-06)
    key_len = jnp.sqrt(key_sq + 1e-06)
    normalized_affinity = gram_raw / (query_len[:, :, None] * key_len[:, None, :])
    normalized_exp_logits = jnp.exp(normalized_affinity * sharpness_factor[:, None, None])
    attention = normalized_exp_logits / lax.optimization_barrier(jnp.sum(normalized_exp_logits, axis=2, keepdims=True))
    attention_b = attention.astype(jnp.bfloat16).astype(jnp.float32)
    attended = jnp.einsum('hij,hjp->hip', attention_b, value_part).astype(jnp.bfloat16)
    flat_out = attended.reshape(channels, pixel_count).astype(jnp.float32)
    flat_dy = upstream_sensitivity.reshape(channels, pixel_count).astype(jnp.float32)
    outgoing_mixer_adjoint = jnp.einsum('op,cp->oc', flat_dy, flat_out)
    grad_attended = jnp.einsum('oc,op->cp', outgoing_mixer.astype(jnp.float32), flat_dy).astype(jnp.bfloat16)
    grad_attended = grad_attended.reshape(group_ordinal, head_size, pixel_count).astype(jnp.float32)
    grad_attention = jnp.einsum('hip,hjp->hij', grad_attended, value_part)
    grad_value = jnp.einsum('hij,hip->hjp', attention_b, grad_attended)
    logits_adjoint = attention * (grad_attention - lax.optimization_barrier(jnp.sum(attention * grad_attention, axis=2, keepdims=True)))
    sharpness_adjoint = lax.optimization_barrier(jnp.sum(logits_adjoint * normalized_affinity, axis=(1, 2)))
    affinity_adjoint = logits_adjoint * sharpness_factor[:, None, None]
    grad_gram = (affinity_adjoint / (query_len[:, :, None] * key_len[:, None, :])).astype(jnp.bfloat16).astype(jnp.float32)
    product_terms = affinity_adjoint * normalized_affinity
    row_terms = lax.optimization_barrier(jnp.sum(product_terms, axis=2))
    col_terms = lax.optimization_barrier(jnp.sum(product_terms, axis=1))
    grad_query = jnp.einsum('hij,hjp->hip', grad_gram, key_part) - query_part * (row_terms / (query_sq + 1e-06))[:, :, None]
    grad_key = jnp.einsum('hij,hip->hjp', grad_gram, query_part) - key_part * (col_terms / (key_sq + 1e-06))[:, :, None]
    grad_mixed = jnp.concatenate([grad_query, grad_key, grad_value], axis=0).reshape(3 * channels, row_count, col_count).astype(jnp.bfloat16)
    grad_padded = jnp.pad(grad_mixed, ((0, 0), (1, 1), (0, 0)))
    grad_projected = depthwise_back(grad_padded, spatial_stencil).astype(jnp.bfloat16)
    spatial_stencil_adjoint = kernel_grad(grad_mixed, padded)
    flat_gproj = grad_projected.reshape(3 * channels, pixel_count).astype(jnp.float32)
    triple_mixer_adjoint = jnp.einsum('op,cp->oc', flat_gproj, normed.reshape(channels, pixel_count).astype(jnp.float32))
    grad_normed = jnp.einsum('oc,op->cp', triple_mixer.astype(jnp.float32), flat_gproj).reshape(channels, row_count, col_count)
    scaling_adjoint = lax.optimization_barrier(jnp.sum(grad_normed * standard, axis=(1, 2)))
    offset_adjoint = lax.optimization_barrier(jnp.sum(grad_normed, axis=(1, 2)))
    scaled = grad_normed * standardize_scaling[:, None, None]
    first_mean = lax.optimization_barrier(jnp.mean(scaled, axis=0, keepdims=True))
    second_mean = lax.optimization_barrier(jnp.mean(scaled * standard, axis=0, keepdims=True))
    feature_map_adjoint = (upstream_sensitivity.astype(jnp.float32) + (scaled - first_mean - standard * second_mean) * inverse).astype(jnp.bfloat16)
    return (feature_map_adjoint, triple_mixer_adjoint, spatial_stencil_adjoint, outgoing_mixer_adjoint, sharpness_adjoint, scaling_adjoint, offset_adjoint)

def reference(block_feature_map, upstream_sensitivity, triple_mixer, spatial_stencil, outgoing_mixer, sharpness_factor, standardize_scaling, standardize_offset):

    def per_image(paired_entries):
        return lone_sample(paired_entries[0], paired_entries[1], triple_mixer, spatial_stencil, outgoing_mixer, sharpness_factor, standardize_scaling, standardize_offset)
    results = lax.map(per_image, (block_feature_map, upstream_sensitivity))
    feature_map_adjoint = results[0]
    return (feature_map_adjoint, lax.optimization_barrier(jnp.sum(results[1], axis=0)), lax.optimization_barrier(jnp.sum(results[2], axis=0)), lax.optimization_barrier(jnp.sum(results[3], axis=0)), lax.optimization_barrier(jnp.sum(results[4], axis=0)), lax.optimization_barrier(jnp.sum(results[5], axis=0)), lax.optimization_barrier(jnp.sum(results[6], axis=0)))
```

```python
import functools

import jax
import jax.numpy as jnp
from jax import lax
from jax.experimental import pallas as pl
from jax.experimental.pallas import tpu as pltpu
from jax.sharding import PartitionSpec as P

F32 = jnp.float32
BF16 = jnp.bfloat16
AXES = ("img", "tile")
NT = (((1,), (1,)), ((), ()))
TN = (((0,), (0,)), ((), ()))
VMEM = pl.BlockSpec(memory_space=pltpu.VMEM)
SMEM = pl.BlockSpec(memory_space=pltpu.SMEM)
HI = lax.Precision.HIGHEST


def params(limit_mib):
    return pltpu.CompilerParams(vmem_limit_bytes=limit_mib << 20)


def call(body, outs, n_in, smem=(), scratch=(), limit=32, flops=0, name=None, moved=0):
    return pl.pallas_call(
        body,
        out_shape=tuple(jax.ShapeDtypeStruct(s, d) for s, d in outs),
        in_specs=[SMEM if i in smem else VMEM for i in range(n_in)],
        out_specs=tuple(VMEM for _ in outs),
        scratch_shapes=list(scratch),
        compiler_params=params(limit),
        cost_estimate=pl.CostEstimate(flops=flops, bytes_accessed=moved, transcendentals=0),
        name=name,
    )


def mm(a, b, dims=None, precision=None):
    dims = dims or (((1,), (0,)), ((), ()))
    return lax.dot_general(a, b, dims, preferred_element_type=F32, precision=precision)


def iota(shape, axis):
    return lax.broadcasted_iota(jnp.int32, shape, axis)


def to_column(row):
    n = row.shape[1]
    eye = iota((n, n), 0) == iota((n, n), 1)
    return jnp.sum(jnp.where(eye, row, 0.0), axis=1, keepdims=True)


def shift_right(v):
    return jnp.where(iota(v.shape, 1) == 0, 0.0, pltpu.roll(v, 1, 1))


def shift_left(v):
    n = v.shape[1]
    return jnp.where(iota(v.shape, 1) == n - 1, 0.0, pltpu.roll(v, n - 1, 1))


def spread_body(x_ref, dy_ref, x2_ref, dy2_ref, up_ref, dn_ref, s):
    c, rows, w = x_ref.shape
    for src, dst, k, off in ((x_ref, x2_ref, 2, 0), (dy_ref, dy2_ref, 1, 2)):
        for i in range(w // 128):
            block = src[:, :, i * 128 : (i + 1) * 128]
            s[i, :, :] = block.astype(F32).reshape(c * rows, 128)
        for h in range(rows):
            v = [s[i, pl.ds(h, c, stride=rows), :] for i in range(w // 128)]
            v = jnp.concatenate(v, axis=1).astype(BF16)
            dst[:, h * w : (h + 1) * w] = v
            if h < k:
                dn_ref[:, (off + h) * w : (off + h + 1) * w] = v
            if h >= rows - k:
                u = off + h - rows + k
                up_ref[:, u * w : (u + 1) * w] = v


def normalise(x, gain, bias):
    average = jnp.mean(x, axis=0, keepdims=True)
    centered = x - average
    inverse = lax.rsqrt(jnp.mean(centered * centered, axis=0, keepdims=True) + 1e-05)
    standard = centered * inverse
    return standard, inverse, (standard * gain + bias).astype(BF16)


def project_body(x2_ref, w_ref, gain_ref, bias_ref, p_ref, std_ref, inv_ref, *, w):
    gain = to_column(gain_ref[...])
    bias = to_column(bias_ref[...])
    for h in range(x2_ref.shape[1] // w):
        at = slice(h * w, (h + 1) * w)
        standard, inverse, normed = normalise(x2_ref[:, at].astype(F32), gain, bias)
        std_ref[:, at] = standard.astype(BF16)
        inv_ref[:, at] = jnp.broadcast_to(inverse, (8, w))
        p_ref[:, at] = mm(w_ref[...], normed).astype(BF16)


def taps_to_columns(taps_ref, wide, coef):
    n = taps_ref.shape[2]
    wide[...] = jnp.zeros_like(wide)
    for a in range(3):
        for b in range(3):
            wide[3 * a + b : 3 * a + b + 1, 0:n] = taps_ref[a, b : b + 1, :]
    coef[...] = wide[...].T


def mix_body(
    flags, p_ref, up_ref, dn_ref, dy2_ref, w_ref, wot_ref, taps_ref, gain_ref, bias_ref,
    mixed_ref, ph_ref, pay_ref, t_ref, wide, coef, sq, gs, *, w, heads,
):
    c3 = p_ref.shape[0]
    c = c3 // 3
    hs = c // heads
    rows = p_ref.shape[1] // w
    gain = to_column(gain_ref[...])
    bias = to_column(bias_ref[...])
    keep_up = 1.0 - flags[0].astype(F32)
    keep_dn = 1.0 - flags[1].astype(F32)
    for src, keep, base in ((up_ref, keep_up, 0), (dn_ref, keep_dn, 2)):
        for h in range(2):
            normed = normalise(src[:, h * w : (h + 1) * w].astype(F32), gain, bias)[2]
            at = slice((base + h) * w, (base + h + 1) * w)
            ph_ref[:, at] = (mm(w_ref[...], normed) * keep).astype(BF16)
    taps_to_columns(taps_ref, wide, coef)

    def group(g, carry):
        ch = pl.ds(pl.multiple_of(g * 16, 16), 16)
        cf = coef[ch, :]
        k = [jnp.broadcast_to(cf[:, t : t + 1], (16, w)) for t in range(9)]

        def row(r):
            if r < 0:
                return ph_ref[ch, (r + 2) * w : (r + 3) * w].astype(F32)
            if r >= rows:
                return ph_ref[ch, (r - rows + 2) * w : (r - rows + 3) * w].astype(F32)
            return p_ref[ch, r * w : (r + 1) * w].astype(F32)

        window = [row(-2), row(-1), None]
        total = jnp.zeros((16, w), F32)
        for r in range(-1, rows + 1):
            window[2] = row(r + 1)
            u = [sum(k[3 * a + b] * window[a] for a in range(3)) for b in range(3)]
            out = (u[1] + shift_right(u[0]) + shift_left(u[2])).astype(BF16)
            mixed_ref[ch, (r + 1) * w : (r + 2) * w] = out
            if 0 <= r < rows:
                out = out.astype(F32)
                total = total + out * out
            window = [window[1], window[2], None]
        sq[ch, :] = jnp.broadcast_to(jnp.sum(total, axis=1, keepdims=True), (16, 128))
        return carry

    lax.fori_loop(0, c3 // 16, group, 0)

    own = slice(w, (rows + 1) * w)
    query = mixed_ref[0:c, own]
    key = mixed_ref[c : 2 * c, own]
    value = mixed_ref[2 * c : 3 * c, own]
    gs[0, :, 0:c] = mm(query, key, NT)
    t = mm(dy2_ref[...], value, NT)
    t_ref[...] = t
    gs[1, :, 0:c] = mm(wot_ref[...].astype(F32), t, precision=HI)
    lane = iota((hs, 128), 1)
    for h in range(heads):
        at = slice(h * hs, (h + 1) * hs)
        gram = pltpu.roll(gs[0, at, :], (256 - hs * h) % 256, 1)[:, 0:128]
        grad = pltpu.roll(gs[1, at, :], (256 + hs - hs * h) % 256, 1)[:, 0:128]
        key_sq = sq[c + h * hs : c + (h + 1) * hs, :]
        rest = jnp.where(lane == 2 * hs, sq[at, :], key_sq)
        pay_ref[at, :] = jnp.where(lane < hs, gram, jnp.where(lane < 2 * hs, grad, rest))


def back_body(
    flags, sharp, mine_ref, other_ref, mixed_ref, p_ref, ph_ref, dy2_ref, up_ref, dn_ref, std_ref,
    t_ref, wot_ref, taps_ref,
    gp_ref, left_ref, right_ref, pay, wide, coef, mats, vecs, gm, aug, grads, *, w, heads,
):
    c = mixed_ref.shape[0] // 3
    hs = c // heads
    rows = p_ref.shape[1] // w
    first_core = flags[3] == 0
    mine = mine_ref[...]
    other = other_ref[...]
    pay[0 : c // 2, :] = jnp.where(first_core, mine, other)
    pay[c // 2 : c, :] = jnp.where(first_core, other, mine)
    lane = iota((hs, 128), 1)
    valid = lane < hs
    eye = lane == iota((hs, 128), 0)
    pad = jnp.zeros((hs, 128), F32)
    sharp_row = jnp.zeros((1, 128), F32)
    for h in range(heads):
        at = slice(h * hs, (h + 1) * hs)
        block = pay[at, :]
        gram = jnp.where(valid, block, 0.0)
        grad = jnp.where(valid, pltpu.roll(block, 128 - hs, 1), 0.0)
        query_sq = block[:, 2 * hs : 2 * hs + 1] + 1e-06
        key_sq = (
            jnp.sum(jnp.where(eye, block[:, 2 * hs + 1 : 2 * hs + 2], 0.0), axis=0, keepdims=True)
            + 1e-06
        )
        length = jnp.sqrt(query_sq) * jnp.sqrt(key_sq)
        cosine = gram / length
        weights = jnp.where(valid, jnp.exp(cosine * sharp[h]), 0.0)
        attention = weights / jnp.sum(weights, axis=1, keepdims=True)
        scores = attention * (grad - jnp.sum(attention * grad, axis=1, keepdims=True))
        terms = scores * cosine
        sharp_h = jnp.sum(jnp.sum(terms, axis=1, keepdims=True), axis=0, keepdims=True)
        sharp_row = jnp.where(iota((1, 128), 1) == h, sharp_h, sharp_row)
        grad_cos = scores * sharp[h]
        terms = grad_cos * cosine
        alpha = jnp.sum(terms, axis=1, keepdims=True) / query_sq
        beta = jnp.sum(terms, axis=0, keepdims=True) / key_sq
        beta = jnp.sum(jnp.where(eye, beta, 0.0), axis=1, keepdims=True)
        vecs[at, 0:128] = jnp.broadcast_to(alpha, (hs, 128))
        vecs[at, 128:256] = jnp.broadcast_to(beta, (hs, 128))
        for i, m in enumerate((grad_cos / length, attention)):
            placed = pltpu.roll(jnp.concatenate([m, pad], axis=1), hs * h, 1)
            mats[i, at, :] = placed.astype(BF16)

    grad_gram = mats[0, :, 0:c]
    grad_gram_t = grad_gram.astype(F32).T.astype(BF16)
    attention_b = mats[1, :, 0:c]
    attention_t = attention_b.astype(F32).T.astype(BF16)
    outgoing = mm(t_ref[...], attention_b.astype(F32), NT, precision=HI)
    alpha = jnp.concatenate([vecs[:, 0:128]] * (w // 128), axis=1)
    beta = jnp.concatenate([vecs[:, 128:256]] * (w // 128), axis=1)
    wot = wot_ref[...]
    for r in range(rows + 2):
        at = slice(r * w, (r + 1) * w)
        if r == 0:
            dy = up_ref[:, 2 * w : 3 * w]
        elif r == rows + 1:
            dy = dn_ref[:, 2 * w : 3 * w]
        else:
            dy = dy2_ref[:, (r - 1) * w : r * w]
        query = mixed_ref[0:c, at]
        key = mixed_ref[c : 2 * c, at]
        grad_attended = mm(wot, dy).astype(BF16)
        parts = (
            mm(grad_gram, key) - query.astype(F32) * alpha,
            mm(grad_gram_t, query) - key.astype(F32) * beta,
            mm(attention_t, grad_attended),
        )
        for i, part in enumerate(parts):
            if r == 0:
                part = part * (1.0 - flags[0].astype(F32))
            if r == rows + 1:
                part = part * (1.0 - flags[1].astype(F32))
            gm[i * c : (i + 1) * c, at] = part.astype(BF16)

    taps_to_columns(taps_ref, wide, coef)

    def group(g, carry):
        ch = pl.ds(pl.multiple_of(g * 16, 16), 16)
        cf = coef[ch, :]
        k = [jnp.broadcast_to(cf[:, t : t + 1], (16, w)) for t in range(9)]
        window = [None, gm[ch, 0:w].astype(F32), gm[ch, w : 2 * w].astype(F32)]
        for r in range(rows):
            window = [window[1], window[2], gm[ch, (r + 2) * w : (r + 3) * w].astype(F32)]
            u = [sum(k[3 * a + b] * window[2 - a] for a in range(3)) for b in range(3)]
            out = u[1] + shift_left(u[0]) + shift_right(u[2])
            gp_ref[ch, r * w : (r + 1) * w] = out.astype(BF16)
        return carry

    lax.fori_loop(0, gm.shape[0] // 16, group, 0)

    def stencil(g, carry):
        ch = pl.ds(pl.multiple_of(g * 16, 16), 16)

        def row(r):
            if r < 0:
                return ph_ref[ch, w : 2 * w].astype(F32)
            if r >= rows:
                return ph_ref[ch, 2 * w : 3 * w].astype(F32)
            return p_ref[ch, r * w : (r + 1) * w].astype(F32)

        acc = [jnp.zeros((16, 128), F32) for _ in range(9)]
        window = [None, row(-1), row(0)]
        for r in range(rows):
            window = [window[1], window[2], row(r + 1)]
            v = gm[ch, (r + 1) * w : (r + 2) * w].astype(F32)
            moved = (shift_left(v), v, shift_right(v))
            for a in range(3):
                for b in range(3):
                    prod = moved[b] * window[a]
                    for i in range(w // 128):
                        acc[3 * a + b] = acc[3 * a + b] + prod[:, i * 128 : (i + 1) * 128]
        lanes = iota((16, 128), 1)
        out = jnp.zeros((16, 128), F32)
        for t in range(9):
            out = jnp.where(lanes == t, jnp.sum(acc[t], axis=1, keepdims=True), out)
        coef[ch, :] = out
        return carry

    lax.fori_loop(0, gm.shape[0] // 16, stencil, 0)

    aug[0:c, :] = std_ref[...]
    aug[c : c + 16, :] = jnp.where(iota((16, rows * w), 0) == 0, 1.0, 0.0).astype(BF16)
    c3 = 3 * c
    grads[...] = jnp.zeros_like(grads)
    grads[0 : c + 16, 0:c3] = mm(aug[...], gp_ref[...], NT)
    grads[c + 16 : c + 32, :] = coef[...].T[0:16, :]
    lead = 1.0 - jnp.minimum(flags[2], 1).astype(F32)
    grads[c + 1 : c + 2, 0:128] = sharp_row * lead
    out_pad = jnp.concatenate([outgoing, jnp.zeros((c, 256 - c), F32)], axis=1)
    half = c3 % 128
    tail = grads[0:c, c3 - half : c3 - half + 128]
    moved = pltpu.roll(out_pad[:, 128:256], half, 1)
    grads[0:c, c3 - half : c3 - half + 128] = jnp.where(iota((c, 128), 1) < half, tail, moved)
    left_ref[...] = grads[:, 0:384].astype(BF16)
    right_ref[:, 0:256] = grads[:, 384:640].astype(BF16)
    right_ref[0:c, 256:384] = out_pad[:, 0:128].astype(BF16)
    right_ref[c : c + 32, 256:384] = jnp.zeros((32, 128), BF16)


def output_body(gp_ref, wt_ref, std_ref, inv_ref, dy_ref, gain_ref, out_ref, s, *, w):
    c, rows, _ = out_ref.shape
    gain = to_column(gain_ref[...])
    for h in range(rows):
        at = slice(h * w, (h + 1) * w)
        scaled = mm(wt_ref[...], gp_ref[:, at]) * gain
        standard = std_ref[:, at].astype(F32)
        first = jnp.mean(scaled, axis=0, keepdims=True)
        second = jnp.mean(scaled * standard, axis=0, keepdims=True)
        v = (scaled - first - standard * second) * inv_ref[0:1, at]
        for i in range(w // 128):
            s[i, pl.ds(h, c, stride=rows), :] = v[:, i * 128 : (i + 1) * 128]
    for i in range(w // 128):
        at = slice(i * 128, (i + 1) * 128)
        v = dy_ref[:, :, at].astype(F32) + s[i, :, :].reshape(c, rows, 128)
        out_ref[:, :, at] = v.astype(BF16)


def finish_body(
    flags, mine_ref, other_ref, wt_ref, gain_ref, bias_ref,
    triple_ref, taps_ref, outgoing_ref, sharp_ref, scaling_ref, offset_ref, full,
):
    c, c3 = wt_ref.shape
    first_core = flags[3] == 0
    mine = mine_ref[...].astype(F32)
    other = other_ref[...].astype(F32)
    full[:, 0:384] = jnp.where(first_core, mine, other)
    full[:, 384:768] = jnp.where(first_core, other, mine)
    m = full[0:c, 0:c3]
    s = full[c : c + 1, 0:c3]
    gain = to_column(gain_ref[...])
    bias = to_column(bias_ref[...])
    wt = wt_ref[...].astype(F32)
    triple_ref[...] = m * gain + bias * s
    eye = iota((c, c), 0) == iota((c, c), 1)
    scaling = jnp.sum(wt * m, axis=1, keepdims=True)
    offset = jnp.sum(wt * s, axis=1, keepdims=True)
    scaling_ref[...] = jnp.sum(jnp.where(eye, scaling, 0.0), axis=0, keepdims=True)
    offset_ref[...] = jnp.sum(jnp.where(eye, offset, 0.0), axis=0, keepdims=True)
    for a in range(3):
        taps_ref[a, :, :] = full[c + 16 + 3 * a : c + 19 + 3 * a, 0:c3]
    half = c3 % 128
    outgoing_ref[:, 0:128] = full[0:c, 640:768]
    tail = pltpu.roll(full[0:c, 512:640], 128 - half, 1)
    outgoing_ref[:, 128:c] = tail[:, 0 : c - 128]
    sharp_ref[...] = full[c + 1 : c + 2, 0:128]


def swap(v, even, odd, count):
    pairs = [(i, i ^ (odd if i & 1 else even)) for i in range(count)]
    return lax.ppermute(v, AXES, pairs)


def rounds(total, tile):
    if total == 256 and tile == 32:
        inner = ((2, 8), (6, 16), (8, 2), (16, 6))
        outer = ((2, 64), (6, 192), (8, 2), (16, 6), (48, 8), (64, 16), (192, 48))
        return inner, outer
    bits = [1 << i for i in range(1, 20)]
    return tuple((b, b) for b in bits if b < tile), tuple((b, b) for b in bits if b < total)


def solution(mesh):
    img, tile = (mesh.shape["img"], mesh.shape["tile"])
    total = img * tile
    inner, outer = rounds(total, tile)

    def local(x, dy, triple, stencil, out_mixer, sharpness, gain, bias):
        _, c, rows, w = x.shape
        heads = sharpness.shape[0]
        c3 = 3 * c
        n = rows * w
        ext = (rows + 2) * w
        place = lax.axis_index("tile")
        core = place % 2
        flags = jnp.stack([place == 0, place == tile - 1, place, core]).astype(jnp.int32)
        x3 = x.reshape(c, rows, w)
        dy3 = dy.reshape(c, rows, w)
        taps = jnp.transpose(stencil, (1, 2, 0))
        wt = triple.T
        wot = out_mixer.T
        gain_row = gain.reshape(1, c)
        bias_row = bias.reshape(1, c)

        x2, dy2, up, dn = call(
            spread_body,
            [((c, n), BF16), ((c, n), BF16), ((c, 3 * w), BF16), ((c, 3 * w), BF16)],
            2,
            scratch=[pltpu.VMEM((w // 128, c * rows, 128), F32)],
            limit=16,
            name="spread",
            moved=4 << 20,
        )(x3, dy3)
        up_in = lax.ppermute(up, "tile", [(i, i + 1) for i in range(tile - 1)])
        dn_in = lax.ppermute(dn, "tile", [(i + 1, i) for i in range(tile - 1)])
        p, std, inv = call(
            functools.partial(project_body, w=w),
            [((c3, n), BF16), ((c, n), BF16), ((8, n), F32)],
            4,
            limit=16,
            flops=2 * c3 * c * n,
            moved=8 << 20,
            name="project",
        )(x2, triple, gain_row, bias_row)
        mixed, ph, pay, t = call(
            functools.partial(mix_body, w=w, heads=heads),
            [((c3, ext), BF16), ((c3, 4 * w), BF16), ((c, 128), F32), ((c, c), F32)],
            10,
            smem=(0,),
            scratch=[
                pltpu.VMEM((128, 640), F32),
                pltpu.VMEM((640, 128), F32),
                pltpu.VMEM((c3, 128), F32),
                pltpu.VMEM((2, c, 256), F32),
            ],
            flops=8 * c * c * n,
            moved=8 << 20,
            name="mix",
        )(flags, p, up_in, dn_in, dy2, triple, wot, taps, gain_row, bias_row)

        half = c // 2
        mine = jnp.where(core == 0, pay[:half], pay[half:])
        theirs = jnp.where(core == 0, pay[half:], pay[:half])
        mine = mine + swap(theirs, 1, 1, total)
        for even, odd in inner:
            mine = mine + swap(mine, even, odd, total)
        other = swap(mine, 1, 1, total)

        gp, left, right = call(
            functools.partial(back_body, w=w, heads=heads),
            [((c3, n), BF16), ((c + 32, 384), BF16), ((c + 32, 384), BF16)],
            14,
            smem=(0, 1),
            scratch=[
                pltpu.VMEM((c, 128), F32),
                pltpu.VMEM((128, 640), F32),
                pltpu.VMEM((640, 128), F32),
                pltpu.VMEM((2, c, 256), BF16),
                pltpu.VMEM((c, 256), F32),
                pltpu.VMEM((c3, ext), BF16),
                pltpu.VMEM((c + 16, n), BF16),
                pltpu.VMEM((c + 32, 640), F32),
            ],
            flops=20 * c * c * n,
            moved=8 << 20,
            name="back",
        )(flags, sharpness, mine, other, mixed, p, ph, dy2, up_in, dn_in, std, t, wot, taps)

        part = jnp.where(core == 0, left, right)
        away = jnp.where(core == 0, right, left)

        def add(a, b):
            return (a.astype(F32) + b.astype(F32)).astype(BF16)

        part = add(part, swap(away, 1, 1, total))
        for even, odd in outer:
            part = add(part, swap(part, even, odd, total))
        rest = swap(part, 1, 1, total)

        (fm,) = call(
            functools.partial(output_body, w=w),
            [((c, rows, w), BF16)],
            6,
            scratch=[pltpu.VMEM((w // 128, c * rows, 128), F32)],
            limit=24,
            flops=2 * c3 * c * n,
            moved=6 << 20,
            name="output",
        )(gp, wt, std, inv, dy3, gain_row)
        outs = call(
            finish_body,
            [((c, c3), F32), ((3, 3, c3), F32), ((c, c), F32), ((1, 128), F32), ((1, c), F32), ((1, c), F32)],
            6,
            smem=(0,),
            scratch=[pltpu.VMEM((c + 32, 768), F32)],
            limit=16,
            name="finish",
            moved=2 << 20,
        )(flags, part, rest, wt, gain_row, bias_row)
        triple_t, taps_t, outgoing, sharp_row, scaling, offset = outs
        return (
            fm.reshape(x.shape),
            triple_t.T,
            jnp.transpose(taps_t, (2, 0, 1)),
            outgoing,
            sharp_row[0, :heads],
            scaling.reshape(c),
            offset.reshape(c),
        )

    return jax.shard_map(
        local,
        mesh=mesh,
        in_specs=(P("img", None, "tile", None), P("img", None, "tile", None)) + (P(),) * 6,
        out_specs=(P("img", None, "tile", None),) + (P(),) * 6,
        check_vma=False,
    )
```

```python
import functools

import jax
import jax.numpy as jnp
from jax import lax
from jax.experimental import pallas as pl
from jax.experimental.pallas import tpu as pltpu
from jax.sharding import Mesh
from jax.sharding import PartitionSpec as P

F32 = jnp.float32
BF16 = jnp.bfloat16
NT = (((1,), (1,)), ((), ()))
TN = (((0,), (0,)), ((), ()))
VMEM = pl.BlockSpec(memory_space=pltpu.VMEM)
SMEM = pl.BlockSpec(memory_space=pltpu.SMEM)
HBM = pl.BlockSpec(memory_space=pltpu.HBM)
HI = lax.Precision.HIGHEST


def params(limit_mib):
    return pltpu.CompilerParams(vmem_limit_bytes=limit_mib << 20)


def call(body, outs, n_in, smem=(), hbm=(), scratch=(), limit=32, flops=0, name=None, moved=0):
    return pl.pallas_call(
        body,
        out_shape=tuple(jax.ShapeDtypeStruct(s, d) for s, d in outs),
        in_specs=[SMEM if i in smem else HBM if i in hbm else VMEM for i in range(n_in)],
        out_specs=tuple(VMEM for _ in outs),
        scratch_shapes=list(scratch),
        compiler_params=params(limit),
        cost_estimate=pl.CostEstimate(flops=flops, bytes_accessed=moved, transcendentals=0),
        name=name,
    )


def mm(a, b, dims=None, precision=None):
    dims = dims or (((1,), (0,)), ((), ()))
    return lax.dot_general(a, b, dims, preferred_element_type=F32, precision=precision)


def iota(shape, axis):
    return lax.broadcasted_iota(jnp.int32, shape, axis)


def to_column(row):
    n = row.shape[1]
    eye = iota((n, n), 0) == iota((n, n), 1)
    return jnp.sum(jnp.where(eye, row, 0.0), axis=1, keepdims=True)


def halves(v):
    return [v[:, i : i + 128] for i in range(0, v.shape[1], 128)]


def joined(parts):
    return jnp.concatenate(parts, axis=1)


def shifters(w):
    row, col = iota((w, w), 0), iota((w, w), 1)
    right = jnp.where(row + 1 == col, 1.0, 0.0)
    left = jnp.where(row == col + 1, 1.0, 0.0)
    return jnp.concatenate([right, left], axis=1).astype(BF16)


def moved_rows(blocks, shift):
    w = blocks[0].shape[1]
    n = blocks[0].shape[0]
    both = mm(jnp.concatenate(blocks, axis=0), shift)
    out = []
    for i, v in enumerate(blocks):
        at = slice(i * n, (i + 1) * n)
        out.append((halves(both[at, 0:w]), [x.astype(F32) for x in halves(v)], halves(both[at, w:])))
    return out


def taps_sum(k, rows, order, i):
    total = None
    for a in range(3):
        for b in range(3):
            term = k[3 * a + b] * rows[order[a]][order[b]][i]
            total = term if total is None else total + term
    return total


def spread_body(flags, x_ref, dy_ref, x2_ref, dy2_ref, up_ref, dn_ref, s):
    c, rows, w = x_ref.shape
    for j, (src, dst, k, off) in enumerate(((x_ref, x2_ref, 2, 0), (dy_ref, dy2_ref, 1, 2))):
        for q in range(w // 128):
            block = src[:, :, q * 128 : (q + 1) * 128]
            s[j, q] = block.astype(F32).reshape(c * rows, 128)
        for h in range(rows):
            v = [s[j, q, pl.ds(h, c, stride=rows), :] for q in range(w // 128)]
            v = jnp.concatenate(v, axis=1).astype(BF16)
            dst[:, h * w : (h + 1) * w] = v
            if h < k:
                dn_ref[:, (off + h) * w : (off + h + 1) * w] = v
            if h >= rows - k:
                u = off + h - rows + k
                up_ref[:, u * w : (u + 1) * w] = v


def columns_body(taps_ref, gain_ref, bias_ref, wt_ref, wo_ref, cols_ref, affine_ref, w_ref, wot_ref, wide):
    n = taps_ref.shape[2]
    c = gain_ref.shape[1]
    wide[...] = jnp.zeros_like(wide)
    for a in range(3):
        for b in range(3):
            wide[3 * a + b : 3 * a + b + 1, 0:n] = taps_ref[a, b : b + 1, :]
    w_ref[...] = wt_ref[...].astype(F32).T.astype(BF16)
    wot_ref[...] = wo_ref[...].astype(F32).T.astype(BF16)
    wide[9:10, 0:c] = gain_ref[...]
    wide[10:11, 0:c] = bias_ref[...]
    for g in range(0, 640, 128):
        flat = wide[:, g : g + 128].T
        m = min(128, n - g)
        for t in range(9):
            cols_ref[t, g : g + m, :] = jnp.broadcast_to(flat[0:m, t : t + 1], (m, 128))
        if g < c:
            m = min(128, c - g)
            for t in range(2):
                affine_ref[t, g : g + m, :] = jnp.broadcast_to(flat[0:m, 9 + t : 10 + t], (m, 128))


def affine(affine_ref, w):
    return [jnp.concatenate([affine_ref[i]] * (w // 128), axis=1) for i in range(2)]


def normalise(x, gain, bias):
    average = jnp.mean(x, axis=0, keepdims=True)
    centered = x - average
    inverse = lax.rsqrt(jnp.mean(centered * centered, axis=0, keepdims=True) + 1e-05)
    standard = centered * inverse
    return standard, inverse, (standard * gain + bias).astype(BF16)


def project_body(x2_ref, w_ref, affine_ref, p_ref, std_ref, inv_ref, *, w):
    gain, bias = affine(affine_ref, w)
    for h in range(x2_ref.shape[1] // w):
        at = slice(h * w, (h + 1) * w)
        standard, inverse, normed = normalise(x2_ref[:, at].astype(F32), gain, bias)
        std_ref[:, at] = standard.astype(BF16)
        inv_ref[:, at] = jnp.broadcast_to(inverse, (8, w))
        p_ref[:, at] = mm(w_ref[...], normed).astype(BF16)


def mix_rows(first, last, row, shift, cols_ref, ch, put):
    k = [cols_ref[t, ch, :] for t in range(9)]
    moved = moved_rows([row(r) for r in range(first - 1, last + 1)], shift)
    for r in range(first, last):
        at = r - first
        put(r, [taps_sum(k, moved[at : at + 3], (0, 1, 2), i) for i in range(len(moved[0][0]))])


def channels(g):
    return pl.ds(pl.multiple_of(g * 16, 16), 16)


def row_reader(p_ref, ph_ref, ch, w):
    rows = p_ref.shape[1] // w

    def row(r):
        if r < 0:
            return ph_ref[ch, (r + 2) * w : (r + 3) * w]
        if r >= rows:
            return ph_ref[ch, (r - rows + 2) * w : (r - rows + 3) * w]
        return p_ref[ch, r * w : (r + 1) * w]

    return row


def mix_body(
    flags, p_ref, up_ref, dn_ref, dy2_ref, w_ref, wot_ref, cols_ref, affine_ref,
    mixed_ref, ph_ref, pay_ref, t_ref, sq, gs, shift, *, w, heads,
):
    c3 = p_ref.shape[0]
    c = c3 // 3
    hs = c // heads
    rows = p_ref.shape[1] // w
    gain, bias = affine(affine_ref, w)
    keep_up = 1.0 - flags[0].astype(F32)
    keep_dn = 1.0 - flags[1].astype(F32)
    shift[...] = shifters(w)
    for src, keep, base in ((up_ref, keep_up, 0), (dn_ref, keep_dn, 2)):
        for h in range(2):
            normed = normalise(src[:, h * w : (h + 1) * w].astype(F32), gain, bias)[2]
            at = slice((base + h) * w, (base + h + 1) * w)
            ph_ref[:, at] = (mm(w_ref[...], normed) * keep).astype(BF16)

    def group(g, carry):
        ch = channels(g)
        total = []

        def put(r, out):
            out = joined(out).astype(BF16)
            mixed_ref[ch, r * w : (r + 1) * w] = out
            for v in halves(out):
                v = v.astype(F32)
                total.append(v * v)
                if len(total) > 1:
                    total[:] = [total[0] + total[1]]

        mix_rows(0, rows, row_reader(p_ref, ph_ref, ch, w), shift[...], cols_ref, ch, put)
        sq[ch, :] = jnp.broadcast_to(jnp.sum(total[0], axis=1, keepdims=True), (16, 128))
        return carry

    lax.fori_loop(0, c3 // 16, group, 0)

    query = mixed_ref[0:c, :]
    key = mixed_ref[c : 2 * c, :]
    value = mixed_ref[2 * c : 3 * c, :]
    gs[0, :, 0:c] = mm(query, key, NT)
    t = mm(dy2_ref[...], value, NT)
    t_ref[...] = t
    gs[1, :, 0:c] = mm(wot_ref[...].astype(F32), t, precision=HI)
    lane = iota((hs, 128), 1)
    for h in range(heads):
        at = slice(h * hs, (h + 1) * hs)
        gram = pltpu.roll(gs[0, at, :], (256 - hs * h) % 256, 1)[:, 0:128]
        grad = pltpu.roll(gs[1, at, :], (256 + hs - hs * h) % 256, 1)[:, 0:128]
        key_sq = sq[c + h * hs : c + (h + 1) * hs, :]
        rest = jnp.where(lane == 2 * hs, sq[at, :], key_sq)
        pay_ref[at, :] = jnp.where(lane < hs, gram, jnp.where(lane < 2 * hs, grad, rest))


def edge_body(p_ref, ph_ref, cols_ref, mh_ref, shift, *, w):
    rows = p_ref.shape[1] // w
    shift[...] = shifters(w)

    def group(g, carry):
        places = [channels(2 * g + part) for part in range(2)]
        edges = (-1, rows)
        blocks = []
        for ch in places:
            row = row_reader(p_ref, ph_ref, ch, w)
            blocks += [row(r + d) for r in edges for d in (-1, 0, 1)]
        moved = moved_rows(blocks, shift[...])
        for j, ch in enumerate(places):
            k = [cols_ref[t, ch, :] for t in range(9)]
            for i in range(2):
                near = moved[6 * j + 3 * i : 6 * j + 3 * i + 3]
                out = [taps_sum(k, near, (0, 1, 2), q) for q in range(w // 128)]
                mh_ref[ch, i * w : (i + 1) * w] = joined(out).astype(BF16)
        return carry

    lax.fori_loop(0, p_ref.shape[0] // 32, group, 0)


def back_body(
    flags, sharp, mine_ref, other_ref, mixed_ref, mh_ref, p_ref, ph_ref, dy2_ref, up_ref, dn_ref,
    std_ref, t_ref, wot_ref, cols_ref,
    gp_ref, left_ref, right_ref, pay, coef, mats, vecs, gm, aug, grads, shift, *, w, heads,
):
    c = mixed_ref.shape[0] // 3
    hs = c // heads
    rows = p_ref.shape[1] // w
    first_core = flags[3] == 0
    mine = mine_ref[...]
    other = other_ref[...]
    pay[0 : c // 2, :] = jnp.where(first_core, mine, other)
    pay[c // 2 : c, :] = jnp.where(first_core, other, mine)
    lane = iota((hs, 128), 1)
    valid = lane < hs
    eye = lane == iota((hs, 128), 0)
    pad = jnp.zeros((hs, 128), F32)
    sharp_row = jnp.zeros((1, 128), F32)
    for h in range(heads):
        at = slice(h * hs, (h + 1) * hs)
        block = pay[at, :]
        gram = jnp.where(valid, block, 0.0)
        grad = jnp.where(valid, pltpu.roll(block, 128 - hs, 1), 0.0)
        query_sq = block[:, 2 * hs : 2 * hs + 1] + 1e-06
        key_sq = (
            jnp.sum(jnp.where(eye, block[:, 2 * hs + 1 : 2 * hs + 2], 0.0), axis=0, keepdims=True)
            + 1e-06
        )
        length = jnp.sqrt(query_sq) * jnp.sqrt(key_sq)
        cosine = gram / length
        weights = jnp.where(valid, jnp.exp(cosine * sharp[h]), 0.0)
        attention = weights / jnp.sum(weights, axis=1, keepdims=True)
        scores = attention * (grad - jnp.sum(attention * grad, axis=1, keepdims=True))
        terms = scores * cosine
        sharp_h = jnp.sum(jnp.sum(terms, axis=1, keepdims=True), axis=0, keepdims=True)
        sharp_row = jnp.where(iota((1, 128), 1) == h, sharp_h, sharp_row)
        grad_cos = scores * sharp[h]
        terms = grad_cos * cosine
        alpha = jnp.sum(terms, axis=1, keepdims=True) / query_sq
        beta = jnp.sum(terms, axis=0, keepdims=True) / key_sq
        beta = jnp.sum(jnp.where(eye, beta, 0.0), axis=1, keepdims=True)
        vecs[at, 0:128] = jnp.broadcast_to(alpha, (hs, 128))
        vecs[at, 128:256] = jnp.broadcast_to(beta, (hs, 128))
        for i, m in enumerate((grad_cos / length, attention)):
            placed = pltpu.roll(jnp.concatenate([m, pad], axis=1), hs * h, 1)
            mats[i, at, :] = placed.astype(BF16)

    grad_gram = mats[0, :, 0:c]
    grad_gram_t = grad_gram.astype(F32).T.astype(BF16)
    attention_b = mats[1, :, 0:c]
    attention_t = attention_b.astype(F32).T.astype(BF16)
    outgoing = mm(t_ref[...], attention_b.astype(F32), NT, precision=HI)
    alpha = jnp.concatenate([vecs[:, 0:128]] * (w // 128), axis=1)
    beta = jnp.concatenate([vecs[:, 128:256]] * (w // 128), axis=1)
    wot = wot_ref[...]
    for r in range(rows + 2):
        at = slice(r * w, (r + 1) * w)
        if r == 0:
            dy = up_ref[:, 2 * w : 3 * w]
            src, own = (mh_ref, slice(0, w))
        elif r == rows + 1:
            dy = dn_ref[:, 2 * w : 3 * w]
            src, own = (mh_ref, slice(w, 2 * w))
        else:
            own = slice((r - 1) * w, r * w)
            dy = dy2_ref[:, own]
            src = mixed_ref
        query = src[0:c, own]
        key = src[c : 2 * c, own]
        grad_attended = mm(wot, dy).astype(BF16)
        parts = (
            mm(grad_gram, key) - query.astype(F32) * alpha,
            mm(grad_gram_t, query) - key.astype(F32) * beta,
            mm(attention_t, grad_attended),
        )
        for i, part in enumerate(parts):
            if r == 0:
                part = part * (1.0 - flags[0].astype(F32))
            if r == rows + 1:
                part = part * (1.0 - flags[1].astype(F32))
            gm[i * c : (i + 1) * c, at] = part.astype(BF16)

    shift[...] = shifters(w)

    def group(g, carry):
        ch = channels(g)
        k = [cols_ref[t, ch, :] for t in range(9)]
        row = row_reader(p_ref, ph_ref, ch, w)
        moved = moved_rows([gm[ch, r * w : (r + 1) * w] for r in range(rows + 2)], shift[...])
        acc = [None] * 9
        window = [None] + [[v.astype(F32) for v in halves(row(r))] for r in (-1, 0)]
        for r in range(rows):
            window = [window[1], window[2], [v.astype(F32) for v in halves(row(r + 1))]]
            parts = range(w // 128)
            out = [taps_sum(k, moved[r : r + 3], (2, 1, 0), i) for i in parts]
            gp_ref[ch, r * w : (r + 1) * w] = joined(out).astype(BF16)
            for a in range(3):
                for b in range(3):
                    t = 3 * a + b
                    for i in parts:
                        term = moved[r + 1][2 - b][i] * window[a][i]
                        acc[t] = term if acc[t] is None else acc[t] + term
        lanes = iota((16, 128), 1)
        out = jnp.zeros((16, 128), F32)
        for t in range(9):
            out = jnp.where(lanes == t, jnp.sum(acc[t], axis=1, keepdims=True), out)
        coef[ch, :] = out
        return carry

    lax.fori_loop(0, gm.shape[0] // 16, group, 0)

    aug[0:c, :] = std_ref[...]
    aug[c : c + 16, :] = jnp.where(iota((16, rows * w), 0) == 0, 1.0, 0.0).astype(BF16)
    c3 = 3 * c
    grads[...] = jnp.zeros_like(grads)
    grads[0 : c + 16, 0:c3] = mm(aug[...], gp_ref[...], NT)
    grads[c + 16 : c + 32, :] = coef[...].T[0:16, :]
    lead = 1.0 - jnp.minimum(flags[2], 1).astype(F32)
    grads[c + 1 : c + 2, 0:128] = sharp_row * lead
    out_pad = jnp.concatenate([outgoing, jnp.zeros((c, 256 - c), F32)], axis=1)
    half = c3 % 128
    tail = grads[0:c, c3 - half : c3 - half + 128]
    moved = pltpu.roll(out_pad[:, 128:256], half, 1)
    grads[0:c, c3 - half : c3 - half + 128] = jnp.where(iota((c, 128), 1) < half, tail, moved)
    left_ref[...] = grads[:, 0:384].astype(BF16)
    right_ref[:, 0:256] = grads[:, 384:640].astype(BF16)
    right_ref[0:c, 256:384] = out_pad[:, 0:128].astype(BF16)
    right_ref[c:, 256:384] = jnp.zeros((grads.shape[0] - c, 128), BF16)


def output_body(gp_ref, wt_ref, std_ref, inv_ref, dy_ref, affine_ref, out_ref, s, *, w):
    c, rows, _ = out_ref.shape
    gain = affine(affine_ref, w)[0]
    for h in range(rows):
        at = slice(h * w, (h + 1) * w)
        scaled = mm(wt_ref[...], gp_ref[:, at]) * gain
        standard = std_ref[:, at].astype(F32)
        first = jnp.mean(scaled, axis=0, keepdims=True)
        second = jnp.mean(scaled * standard, axis=0, keepdims=True)
        v = (scaled - first - standard * second) * inv_ref[0:1, at]
        for i in range(w // 128):
            s[i, pl.ds(h, c, stride=rows), :] = v[:, i * 128 : (i + 1) * 128]
    for i in range(w // 128):
        at = slice(i * 128, (i + 1) * 128)
        v = dy_ref[:, :, at].astype(F32) + s[i, :, :].reshape(c, rows, 128)
        out_ref[:, :, at] = v.astype(BF16)


def finish_body(
    flags, mine_ref, other_ref, wt_ref, gain_ref, bias_ref,
    triple_ref, taps_ref, outgoing_ref, sharp_ref, scaling_ref, offset_ref, full,
):
    c, c3 = wt_ref.shape
    first_core = flags[3] == 0
    mine = mine_ref[...].astype(F32)
    other = other_ref[...].astype(F32)
    full[:, 0:384] = jnp.where(first_core, mine, other)
    full[:, 384:768] = jnp.where(first_core, other, mine)
    m = full[0:c, 0:c3]
    s = full[c : c + 1, 0:c3]
    gain = to_column(gain_ref[...])
    bias = to_column(bias_ref[...])
    wt = wt_ref[...].astype(F32)
    triple_ref[...] = m * gain + bias * s
    eye = iota((c, c), 0) == iota((c, c), 1)
    scaling = jnp.sum(wt * m, axis=1, keepdims=True)
    offset = jnp.sum(wt * s, axis=1, keepdims=True)
    scaling_ref[...] = jnp.sum(jnp.where(eye, scaling, 0.0), axis=0, keepdims=True)
    offset_ref[...] = jnp.sum(jnp.where(eye, offset, 0.0), axis=0, keepdims=True)
    for a in range(3):
        taps_ref[a, :, :] = full[c + 16 + 3 * a : c + 19 + 3 * a, 0:c3]
    half = c3 % 128
    outgoing_ref[:, 0:128] = full[0:c, 640:768]
    tail = pltpu.roll(full[0:c, 512:640], 128 - half, 1)
    outgoing_ref[:, 128:c] = tail[:, 0 : c - 128]
    sharp_ref[...] = full[c + 1 : c + 2, 0 : sharp_ref.shape[1]]


GROUP = ("img", "chip")
ALL = ("img", "chip", "core")


def swap(v, mask, count):
    return lax.ppermute(v, ALL, [(i, i ^ mask) for i in range(count)])


def bits(total, tile):
    if total == 256 and tile == 32:
        return (2, 6, 8, 16)
    return tuple(1 << i for i in range(1, 20) if 1 << i < tile)


def solution(mesh):
    img, tile = (mesh.shape["img"], mesh.shape["tile"])
    total = img * tile
    chips = total // 2
    mesh = Mesh(mesh.devices.reshape(img, tile // 2, 2), ALL)
    strip = ("chip", "core")

    def local(x, dy, triple, stencil, out_mixer, sharpness, gain, bias):
        _, c, rows, w = x.shape
        heads = sharpness.shape[0]
        c3 = 3 * c
        n = rows * w
        core = lax.axis_index("core")
        place = lax.axis_index("chip") * 2 + core
        flags = jnp.stack([place == 0, place == tile - 1, place, core]).astype(jnp.int32)
        x3 = x.reshape(c, rows, w)
        dy3 = dy.reshape(c, rows, w)
        taps = jnp.transpose(stencil, (1, 2, 0))
        wt = triple.T
        gain_row = gain.reshape(1, c)
        bias_row = bias.reshape(1, c)

        x2, dy2, up, dn = call(
            spread_body,
            [((c, n), BF16), ((c, n), BF16), ((c, 3 * w), BF16), ((c, 3 * w), BF16)],
            3,
            smem=(0,),
            scratch=[pltpu.VMEM((2, w // 128, c * rows, 128), F32)],
            limit=8,
            name="spread",
            moved=4 << 20,
        )(flags, x3, dy3)
        even = core == 0
        inside = lax.ppermute(jnp.where(even, up, dn), strip, [(i, i ^ 1) for i in range(tile)])
        pairs = [(i, i + 1) for i in range(1, tile - 1, 2)]
        across = jnp.where(even, dn, up)
        across = lax.ppermute(across, strip, pairs + [(j, i) for i, j in pairs])
        cols, aff, w_row, wot = call(
            columns_body,
            [((9, c3, 128), F32), ((2, c, 128), F32), ((c3, c), BF16), ((c, c), BF16)],
            5,
            scratch=[pltpu.VMEM((128, 640), F32)],
            limit=16,
            moved=4 << 20,
            name="columns",
        )(taps, gain_row, bias_row, wt, out_mixer)
        p, std, inv = call(
            functools.partial(project_body, w=w),
            [((c3, n), BF16), ((c, n), BF16), ((8, n), F32)],
            3,
            limit=16,
            flops=2 * c3 * c * n,
            moved=8 << 20,
            name="project",
        )(x2, w_row, aff)
        up_in = jnp.where(even, across, inside)
        dn_in = jnp.where(even, inside, across)
        mixed, ph, pay, t = call(
            functools.partial(mix_body, w=w, heads=heads),
            [((c3, n), BF16), ((c3, 4 * w), BF16), ((c, 128), F32), ((c, c), F32)],
            9,
            smem=(0,),
            scratch=[
                pltpu.VMEM((c3, 128), F32),
                pltpu.VMEM((2, c, 256), F32),
                pltpu.VMEM((w, 2 * w), BF16),
            ],
            limit=12,
            flops=8 * c * c * n,
            moved=8 << 20,
            name="mix",
        )(flags, p, up_in, dn_in, dy2, w_row, wot, cols, aff)

        half = c // 2
        mine = jnp.where(core == 0, pay[:half], pay[half:])
        theirs = jnp.where(core == 0, pay[half:], pay[:half])
        mine = mine + swap(theirs, 1, total)
        (mh,) = call(
            functools.partial(edge_body, w=w),
            [((c3, 2 * w), BF16)],
            3,
            scratch=[pltpu.VMEM((w, 2 * w), BF16)],
            limit=8,
            moved=6 << 20,
            name="edge",
        )(p, ph, cols)
        for i, mask in enumerate(bits(total, tile)):
            mine = mine + swap(mine, mask, total)
            if i == 0:
                mine, mh = lax.optimization_barrier((mine, mh))
        other = swap(mine, 1, total)

        each = pl.cdiv(c + 32, 2 * chips) * 2
        size = each * chips
        gp, left, right = call(
            functools.partial(back_body, w=w, heads=heads),
            [((c3, n), BF16), ((size, 384), BF16), ((size, 384), BF16)],
            15,
            smem=(0, 1),
            scratch=[
                pltpu.VMEM((c, 128), F32),
                pltpu.VMEM((640, 128), F32),
                pltpu.VMEM((2, c, 256), BF16),
                pltpu.VMEM((c, 256), F32),
                pltpu.VMEM((c3, (rows + 2) * w), BF16),
                pltpu.VMEM((c + 16, n), BF16),
                pltpu.VMEM((size, 640), F32),
                pltpu.VMEM((w, 2 * w), BF16),
            ],
            limit=20,
            flops=20 * c * c * n,
            moved=8 << 20,
            name="back",
        )(flags, sharpness, mine, other, mixed, mh, p, ph, dy2, up_in, dn_in, std, t, wot, cols)

        (fm,) = call(
            functools.partial(output_body, w=w),
            [((c, rows, w), BF16)],
            6,
            scratch=[pltpu.VMEM((w // 128, c * rows, 128), F32)],
            limit=10,
            flops=2 * c3 * c * n,
            moved=6 << 20,
            name="output",
        )(gp, wt, std, inv, dy3, aff)
        part = jnp.where(core == 0, left, right)
        away = jnp.where(core == 0, right, left)
        part = (part.astype(F32) + swap(away, 1, total).astype(F32)).astype(BF16)
        got = lax.all_to_all(part.reshape(chips, each, 384), GROUP, 0, 0)
        piece = jnp.sum(got.astype(F32), axis=0, keepdims=True).astype(BF16)
        piece, fm = lax.optimization_barrier((piece, fm))
        part = lax.all_to_all(jnp.broadcast_to(piece, got.shape), GROUP, 0, 0)
        part = part.reshape(size, 384)
        rest = swap(part, 1, total)

        outs = call(
            finish_body,
            [((c, c3), F32), ((3, 3, c3), F32), ((c, c), F32), ((1, heads), F32), ((1, c), F32), ((1, c), F32)],
            6,
            smem=(0,),
            scratch=[pltpu.VMEM((size, 768), F32)],
            limit=16,
            name="finish",
            moved=2 << 20,
        )(flags, part, rest, wt, gain_row, bias_row)
        triple_t, taps_t, outgoing, sharp_row, scaling, offset = outs
        return (
            fm.reshape(x.shape),
            triple_t.T,
            jnp.transpose(taps_t, (2, 0, 1)),
            outgoing,
            sharp_row.reshape(heads),
            scaling.reshape(c),
            offset.reshape(c),
        )

    return jax.shard_map(
        local,
        mesh=mesh,
        in_specs=(P("img", None, strip, None), P("img", None, strip, None)) + (P(),) * 6,
        out_specs=(P("img", None, strip, None),) + (P(),) * 6,
        check_vma=False,
    )
```

```python
import functools

import jax
import jax.numpy as jnp
from jax import lax
from jax.experimental import pallas as pl
from jax.experimental.pallas import tpu as pltpu
from jax.sharding import Mesh
from jax.sharding import PartitionSpec as P

F32 = jnp.float32
BF16 = jnp.bfloat16
NT = (((1,), (1,)), ((), ()))
TN = (((0,), (0,)), ((), ()))
VMEM = pl.BlockSpec(memory_space=pltpu.VMEM)
HBM = pl.BlockSpec(memory_space=pltpu.HBM)
HI = lax.Precision.HIGHEST


def params(limit_mib):
    return pltpu.CompilerParams(vmem_limit_bytes=limit_mib << 20)


def call(body, outs, n_in, hbm_out=(), scratch=(), limit=32, flops=0, name=None, moved=0):
    return pl.pallas_call(
        body,
        out_shape=tuple(jax.ShapeDtypeStruct(s, d) for s, d in outs),
        in_specs=[VMEM for _ in range(n_in)],
        out_specs=tuple(HBM if i in hbm_out else VMEM for i in range(len(outs))),
        scratch_shapes=list(scratch),
        compiler_params=params(limit),
        cost_estimate=pl.CostEstimate(flops=flops, bytes_accessed=moved, transcendentals=0),
        name=name,
    )


def mm(a, b, dims=None, precision=None):
    dims = dims or (((1,), (0,)), ((), ()))
    return lax.dot_general(a, b, dims, preferred_element_type=F32, precision=precision)


def iota(shape, axis):
    return lax.broadcasted_iota(jnp.int32, shape, axis)


def to_column(row):
    n = row.shape[1]
    eye = iota((n, n), 0) == iota((n, n), 1)
    return jnp.sum(jnp.where(eye, row, 0.0), axis=1, keepdims=True)


def halves(v):
    return [v[:, i : i + 128] for i in range(0, v.shape[1], 128)]


def joined(parts):
    return jnp.concatenate(parts, axis=1)


def shift_right(parts):
    first = iota(parts[0].shape, 1) == 0
    moved = [pltpu.roll(p, 1, 1) for p in parts]
    before = [jnp.zeros_like(parts[0])] + moved[:-1]
    return [jnp.where(first, b, m) for b, m in zip(before, moved)]


def shift_left(parts):
    last = iota(parts[0].shape, 1) == 127
    moved = [pltpu.roll(p, 127, 1) for p in parts]
    after = moved[1:] + [jnp.zeros_like(parts[0])]
    return [jnp.where(last, a, m) for a, m in zip(after, moved)]


def combine(k, window, order):
    count = range(len(window[0]))
    return [
        [sum(k[3 * a + b] * window[order[a]][i] for a in range(3)) for i in count]
        for b in range(3)
    ]


def each_group(total, body, batch=6):
    def trip(g, carry):
        for j in range(batch):
            body(pl.ds(pl.multiple_of((g * batch + j) * 16, 16), 16))
        return carry

    lax.fori_loop(0, total // (16 * batch), trip, 0)


def spread_body(flags, x_ref, dy_ref, x2_ref, dy2_ref, up_ref, dn_ref, s):
    c, rows, w = x_ref.shape
    for j, (src, dst, k, off) in enumerate(((x_ref, x2_ref, 2, 0), (dy_ref, dy2_ref, 1, 2))):
        for q in range(w // 128):
            block = src[:, :, q * 128 : (q + 1) * 128]
            s[j, q] = block.astype(F32).reshape(c * rows, 128)
        for h in range(rows):
            v = [s[j, q, pl.ds(h, c, stride=rows), :] for q in range(w // 128)]
            v = jnp.concatenate(v, axis=1).astype(BF16)
            dst[:, h * w : (h + 1) * w] = v
            if h < k:
                dn_ref[:, (off + h) * w : (off + h + 1) * w] = v
            if h >= rows - k:
                u = off + h - rows + k
                up_ref[:, u * w : (u + 1) * w] = v


def columns_body(taps_ref, gain_ref, bias_ref, wt_ref, wo_ref, cols_ref, affine_ref, w_ref, wot_ref, wide):
    n = taps_ref.shape[2]
    c = gain_ref.shape[1]
    wide[...] = jnp.zeros_like(wide)
    for a in range(3):
        for b in range(3):
            wide[3 * a + b : 3 * a + b + 1, 0:n] = taps_ref[a, b : b + 1, :]
    w_ref[...] = wt_ref[...].astype(F32).T.astype(BF16)
    wot_ref[...] = wo_ref[...].astype(F32).T.astype(BF16)
    wide[9:10, 0:c] = gain_ref[...]
    wide[10:11, 0:c] = bias_ref[...]
    for g in range(0, 640, 128):
        flat = wide[:, g : g + 128].T
        m = min(128, n - g)
        for t in range(9):
            cols_ref[t, g : g + m, :] = jnp.broadcast_to(flat[0:m, t : t + 1], (m, 128))
        if g < c:
            m = min(128, c - g)
            for t in range(2):
                affine_ref[t, g : g + m, :] = jnp.broadcast_to(flat[0:m, 9 + t : 10 + t], (m, 128))


def affine(affine_ref, w):
    return [jnp.concatenate([affine_ref[i]] * (w // 128), axis=1) for i in range(2)]


def normalise(x, gain, bias):
    average = jnp.mean(x, axis=0, keepdims=True)
    centered = x - average
    inverse = lax.rsqrt(jnp.mean(centered * centered, axis=0, keepdims=True) + 1e-05)
    standard = centered * inverse
    return standard, inverse, (standard * gain + bias).astype(BF16)


def project_body(x2_ref, w_ref, affine_ref, p_ref, std_ref, inv_ref, *, w):
    gain, bias = affine(affine_ref, w)
    for h in range(x2_ref.shape[1] // w):
        at = slice(h * w, (h + 1) * w)
        standard, inverse, normed = normalise(x2_ref[:, at].astype(F32), gain, bias)
        std_ref[:, at] = standard.astype(BF16)
        inv_ref[:, at] = jnp.broadcast_to(inverse, (8, w))
        p_ref[:, at] = mm(w_ref[...], normed).astype(BF16)


def mix_rows(first, last, row, cols_ref, ch, put):
    k = [cols_ref[t, ch, :] for t in range(9)]
    window = [row(first - 1), row(first), None]
    for r in range(first, last):
        window[2] = row(r + 1)
        u = combine(k, window, (0, 1, 2))
        put(r, [x + y + z for x, y, z in zip(u[1], shift_right(u[0]), shift_left(u[2]))])
        window = [window[1], window[2], None]


def row_reader(p_ref, ph_ref, ch, w):
    rows = p_ref.shape[1] // w

    def row(r):
        if r < 0:
            return ph_ref[ch, (r + 2) * w : (r + 3) * w]
        if r >= rows:
            return ph_ref[ch, (r - rows + 2) * w : (r - rows + 3) * w]
        return p_ref[ch, r * w : (r + 1) * w]

    return row


def wide_reader(p_ref, ph_ref, ch, w):
    row = row_reader(p_ref, ph_ref, ch, w)
    return lambda r: [v.astype(F32) for v in halves(row(r))]


def mix_body(
    flags, p_ref, up_ref, dn_ref, dy2_ref, w_ref, wot_ref, cols_ref, affine_ref,
    mixed_ref, ph_ref, pay_ref, t_ref, sq, gs, *, w, heads,
):
    c3 = p_ref.shape[0]
    c = c3 // 3
    hs = c // heads
    rows = p_ref.shape[1] // w
    gain, bias = affine(affine_ref, w)
    keep_up = flags[0:1, 0:1]
    keep_dn = flags[1:2, 0:1]
    for src, keep, base in ((up_ref, keep_up, 0), (dn_ref, keep_dn, 2)):
        for h in range(2):
            normed = normalise(src[:, h * w : (h + 1) * w].astype(F32), gain, bias)[2]
            at = slice((base + h) * w, (base + h + 1) * w)
            ph_ref[:, at] = (mm(w_ref[...], normed) * keep).astype(BF16)

    def group(ch):
        total = []

        def put(r, out):
            out = joined(out).astype(BF16)
            mixed_ref[ch, r * w : (r + 1) * w] = out
            for v in halves(out):
                v = v.astype(F32)
                total.append(v * v)
                if len(total) > 1:
                    total[:] = [total[0] + total[1]]

        mix_rows(0, rows, wide_reader(p_ref, ph_ref, ch, w), cols_ref, ch, put)
        sq[ch, :] = total[0]

    each_group(c3, group)

    query = mixed_ref[0:c, :]
    key = mixed_ref[c : 2 * c, :]
    value = mixed_ref[2 * c : 3 * c, :]
    gs[0, :, 0:c] = mm(query, key, NT)
    t = mm(dy2_ref[...], value, NT)
    t_ref[...] = t
    gs[1, :, 0:c] = mm(wot_ref[...].astype(F32), t, precision=HI)
    lane = iota((hs, 128), 1)
    for h in range(heads):
        at = slice(h * hs, (h + 1) * hs)
        gram = pltpu.roll(gs[0, at, :], (256 - hs * h) % 256, 1)[:, 0:128]
        grad = pltpu.roll(gs[1, at, :], (256 + hs - hs * h) % 256, 1)[:, 0:128]
        query_sq = jnp.sum(sq[at, :], axis=1, keepdims=True)
        key_sq = jnp.sum(sq[c + h * hs : c + (h + 1) * hs, :], axis=1, keepdims=True)
        rest = jnp.where(lane == 2 * hs, query_sq, key_sq)
        pay_ref[at, :] = jnp.where(lane < hs, gram, jnp.where(lane < 2 * hs, grad, rest))


def edge_body(p_ref, ph_ref, cols_ref, mh_ref, *, w):
    rows = p_ref.shape[1] // w

    def group(ch):
        row = wide_reader(p_ref, ph_ref, ch, w)
        for i, r in enumerate((-1, rows)):
            def put(_, out):
                mh_ref[ch, i * w : (i + 1) * w] = joined(out).astype(BF16)

            mix_rows(r, r + 1, row, cols_ref, ch, put)

    each_group(p_ref.shape[0], group)


def back_body(
    flags, sharp, mine_ref, other_ref, mixed_ref, mh_ref, p_ref, ph_ref, dy2_ref, up_ref, dn_ref,
    std_ref, t_ref, wot_ref, cols_ref,
    gp_hbm, left_ref, right_ref, pay, coef, sums, mats, vecs, gm, aug, grads, gp_ref, sem, *, w, heads,
):
    c = mixed_ref.shape[0] // 3
    hs = c // heads
    rows = p_ref.shape[1] // w
    mine = mine_ref[...]
    other = other_ref[...]
    first_core = jnp.broadcast_to(flags[3:4, :], mine.shape) < 0.5
    pay[0 : c // 2, :] = jnp.where(first_core, mine, other)
    pay[c // 2 : c, :] = jnp.where(first_core, other, mine)
    lane = iota((hs, 128), 1)
    valid = lane < hs
    eye = lane == iota((hs, 128), 0)
    pad = jnp.zeros((hs, 128), F32)
    sharp_row = jnp.zeros((1, 128), F32)
    for h in range(heads):
        at = slice(h * hs, (h + 1) * hs)
        block = pay[at, :]
        gram = jnp.where(valid, block, 0.0)
        grad = jnp.where(valid, pltpu.roll(block, 128 - hs, 1), 0.0)
        query_sq = block[:, 2 * hs : 2 * hs + 1] + 1e-06
        key_sq = (
            jnp.sum(jnp.where(eye, block[:, 2 * hs + 1 : 2 * hs + 2], 0.0), axis=0, keepdims=True)
            + 1e-06
        )
        length = jnp.sqrt(query_sq) * jnp.sqrt(key_sq)
        cosine = gram / length
        weights = jnp.where(valid, jnp.exp(cosine * sharp[0:1, h : h + 1]), 0.0)
        attention = weights / jnp.sum(weights, axis=1, keepdims=True)
        scores = attention * (grad - jnp.sum(attention * grad, axis=1, keepdims=True))
        terms = scores * cosine
        sharp_h = jnp.sum(jnp.sum(terms, axis=1, keepdims=True), axis=0, keepdims=True)
        sharp_row = jnp.where(iota((1, 128), 1) == h, sharp_h, sharp_row)
        grad_cos = scores * sharp[0:1, h : h + 1]
        terms = grad_cos * cosine
        alpha = jnp.sum(terms, axis=1, keepdims=True) / query_sq
        beta = jnp.sum(terms, axis=0, keepdims=True) / key_sq
        beta = jnp.sum(jnp.where(eye, beta, 0.0), axis=1, keepdims=True)
        vecs[at, 0:128] = jnp.broadcast_to(alpha, (hs, 128))
        vecs[at, 128:256] = jnp.broadcast_to(beta, (hs, 128))
        for i, m in enumerate((grad_cos / length, attention)):
            placed = pltpu.roll(jnp.concatenate([m, pad], axis=1), hs * h, 1)
            mats[i, at, :] = placed.astype(BF16)

    grad_gram = mats[0, :, 0:c]
    grad_gram_t = grad_gram.astype(F32).T.astype(BF16)
    attention_b = mats[1, :, 0:c]
    attention_t = attention_b.astype(F32).T.astype(BF16)
    outgoing = mm(t_ref[...], attention_b.astype(F32), NT, precision=HI)
    alpha = jnp.concatenate([vecs[:, 0:128]] * (w // 128), axis=1)
    beta = jnp.concatenate([vecs[:, 128:256]] * (w // 128), axis=1)
    wot = wot_ref[...]
    for r in range(rows + 2):
        at = slice(r * w, (r + 1) * w)
        if r == 0:
            dy = up_ref[:, 2 * w : 3 * w]
            src, own = (mh_ref, slice(0, w))
        elif r == rows + 1:
            dy = dn_ref[:, 2 * w : 3 * w]
            src, own = (mh_ref, slice(w, 2 * w))
        else:
            own = slice((r - 1) * w, r * w)
            dy = dy2_ref[:, own]
            src = mixed_ref
        query = src[0:c, own]
        key = src[c : 2 * c, own]
        grad_attended = mm(wot, dy).astype(BF16)
        parts = (
            mm(grad_gram, key) - query.astype(F32) * alpha,
            mm(grad_gram_t, query) - key.astype(F32) * beta,
            mm(attention_t, grad_attended),
        )
        for i, part in enumerate(parts):
            if r == 0:
                part = part * flags[0:1, 0:1]
            if r == rows + 1:
                part = part * flags[1:2, 0:1]
            gm[i * c : (i + 1) * c, at] = part.astype(BF16)

    def input_grad(ch):
        k = [cols_ref[t, ch, :] for t in range(9)]

        def row(r):
            return [v.astype(F32) for v in halves(gm[ch, r * w : (r + 1) * w])]

        window = [None, row(0), row(1)]
        for r in range(rows):
            window = [window[1], window[2], row(r + 2)]
            u = combine(k, window, (2, 1, 0))
            out = [x + y + z for x, y, z in zip(u[1], shift_left(u[0]), shift_right(u[2]))]
            gp_ref[ch, r * w : (r + 1) * w] = joined(out).astype(BF16)

    each_group(3 * c, input_grad)
    copies = []
    for i in range(3):
        at = pl.ds(i * c, c)
        copies.append(pltpu.make_async_copy(gp_ref.at[at], gp_hbm.at[at], sem.at[i]))
        copies[-1].start()

    def stencil(ch):
        row = wide_reader(p_ref, ph_ref, ch, w)
        acc = [None] * 9
        window = [None, row(-1), row(0)]
        for r in range(rows):
            window = [window[1], window[2], row(r + 1)]
            v = [x.astype(F32) for x in halves(gm[ch, (r + 1) * w : (r + 2) * w])]
            moved = (shift_left(v), v, shift_right(v))
            for t in range(9):
                for x, y in zip(moved[t % 3], window[t // 3]):
                    acc[t] = x * y if acc[t] is None else acc[t] + x * y
        for t in range(9):
            sums[ch, t * 128 : (t + 1) * 128] = acc[t]

    each_group(3 * c, stencil)
    place = iota((9 * 128, 128), 0) // 128 == iota((9 * 128, 128), 1)
    place = jnp.where(place, 1.0, 0.0).astype(BF16)
    for g in range(0, 3 * c, 64):
        block = sums[g : g + 64, :]
        high = block.astype(BF16)
        low = (block - high.astype(F32)).astype(BF16)
        coef[g : g + 64, :] = mm(high, place) + mm(low, place)

    aug[0:c, :] = std_ref[...]
    aug[c : c + 16, :] = jnp.where(iota((16, rows * w), 0) == 0, 1.0, 0.0).astype(BF16)
    c3 = 3 * c
    grads[...] = jnp.zeros_like(grads)
    grads[0 : c + 16, 0:c3] = mm(aug[...], gp_ref[...], NT)
    grads[c + 16 : c + 32, :] = coef[...].T[0:16, :]
    grads[c + 1 : c + 2, 0:128] = sharp_row * flags[2:3, :]
    out_pad = jnp.concatenate([outgoing, jnp.zeros((c, 256 - c), F32)], axis=1)
    half = c3 % 128
    tail = grads[0:c, c3 - half : c3 - half + 128]
    moved = pltpu.roll(out_pad[:, 128:256], half, 1)
    grads[0:c, c3 - half : c3 - half + 128] = jnp.where(iota((c, 128), 1) < half, tail, moved)
    left_ref[...] = grads[:, 0:384].astype(BF16)
    right_ref[:, 0:256] = grads[:, 384:640].astype(BF16)
    right_ref[0:c, 256:384] = out_pad[:, 0:128].astype(BF16)
    right_ref[c:, 256:384] = jnp.zeros((grads.shape[0] - c, 128), BF16)
    for copy in copies:
        copy.wait()


def output_body(gp_ref, wt_ref, std_ref, inv_ref, dy_ref, affine_ref, out_ref, s, *, w):
    c, rows, _ = out_ref.shape
    gain = affine(affine_ref, w)[0]
    for h in range(rows):
        at = slice(h * w, (h + 1) * w)
        scaled = mm(wt_ref[...], gp_ref[:, at]) * gain
        standard = std_ref[:, at].astype(F32)
        first = jnp.mean(scaled, axis=0, keepdims=True)
        second = jnp.mean(scaled * standard, axis=0, keepdims=True)
        v = (scaled - first - standard * second) * inv_ref[0:1, at]
        for i in range(w // 128):
            s[i, pl.ds(h, c, stride=rows), :] = v[:, i * 128 : (i + 1) * 128]
    for i in range(w // 128):
        at = slice(i * 128, (i + 1) * 128)
        v = dy_ref[:, :, at].astype(F32) + s[i, :, :].reshape(c, rows, 128)
        out_ref[:, :, at] = v.astype(BF16)


def finish_body(
    flags, mine_ref, other_ref, wt_ref, gain_ref, bias_ref,
    triple_ref, taps_ref, outgoing_ref, sharp_ref, scaling_ref, offset_ref, full,
):
    c, c3 = wt_ref.shape
    mine = mine_ref[...].astype(F32)
    other = other_ref[...].astype(F32)
    first_core = jnp.broadcast_to(flags[3:4, 0:1], mine.shape) < 0.5
    full[:, 0:384] = jnp.where(first_core, mine, other)
    full[:, 384:768] = jnp.where(first_core, other, mine)
    m = full[0:c, 0:c3]
    s = full[c : c + 1, 0:c3]
    gain = to_column(gain_ref[...])
    bias = to_column(bias_ref[...])
    wt = wt_ref[...].astype(F32)
    triple_ref[...] = m * gain + bias * s
    eye = iota((c, c), 0) == iota((c, c), 1)
    scaling = jnp.sum(wt * m, axis=1, keepdims=True)
    offset = jnp.sum(wt * s, axis=1, keepdims=True)
    scaling_ref[...] = jnp.sum(jnp.where(eye, scaling, 0.0), axis=0, keepdims=True)
    offset_ref[...] = jnp.sum(jnp.where(eye, offset, 0.0), axis=0, keepdims=True)
    for a in range(3):
        taps_ref[a, :, :] = full[c + 16 + 3 * a : c + 19 + 3 * a, 0:c3]
    half = c3 % 128
    outgoing_ref[:, 0:128] = full[0:c, 640:768]
    tail = pltpu.roll(full[0:c, 512:640], 128 - half, 1)
    outgoing_ref[:, 128:c] = tail[:, 0 : c - 128]
    sharp_ref[...] = full[c + 1 : c + 2, 0 : sharp_ref.shape[1]]


GROUP = ("img", "chip")
ALL = ("img", "chip", "core")


def swap(v, mask, count):
    return lax.ppermute(v, ALL, [(i, i ^ mask) for i in range(count)])


def bits(total, tile):
    if total == 256 and tile == 32:
        return (2, 6, 8, 16)
    return tuple(1 << i for i in range(1, 20) if 1 << i < tile)


def solution(mesh):
    img, tile = (mesh.shape["img"], mesh.shape["tile"])
    total = img * tile
    chips = total // 2
    mesh = Mesh(mesh.devices.reshape(img, tile // 2, 2), ALL)
    strip = ("chip", "core")

    def local(x, dy, triple, stencil, out_mixer, sharpness, gain, bias):
        _, c, rows, w = x.shape
        heads = sharpness.shape[0]
        c3 = 3 * c
        n = rows * w
        core = lax.axis_index("core")
        place = lax.axis_index("chip") * 2 + core
        flags = jnp.stack([place != 0, place != tile - 1, place == 0, core == 1]).astype(F32)
        flags = jnp.broadcast_to(jnp.pad(flags, (0, 4))[:, None], (8, 128))
        x3 = x.reshape(c, rows, w)
        dy3 = dy.reshape(c, rows, w)
        taps = jnp.transpose(stencil, (1, 2, 0))
        wt = triple.T
        gain_row = gain.reshape(1, c)
        bias_row = bias.reshape(1, c)

        x2, dy2, up, dn = call(
            spread_body,
            [((c, n), BF16), ((c, n), BF16), ((c, 3 * w), BF16), ((c, 3 * w), BF16)],
            3,
            scratch=[pltpu.VMEM((2, w // 128, c * rows, 128), F32)],
            limit=8,
            name="spread",
            moved=4 << 20,
        )(flags, x3, dy3)
        even = core == 0
        inside = lax.ppermute(jnp.where(even, up, dn), strip, [(i, i ^ 1) for i in range(tile)])
        pairs = [(i, i + 1) for i in range(1, tile - 1, 2)]
        across = jnp.where(even, dn, up)
        across = lax.ppermute(across, strip, pairs + [(j, i) for i, j in pairs])
        cols, aff, w_row, wot = call(
            columns_body,
            [((9, c3, 128), F32), ((2, c, 128), F32), ((c3, c), BF16), ((c, c), BF16)],
            5,
            scratch=[pltpu.VMEM((128, 640), F32)],
            limit=16,
            moved=4 << 20,
            name="columns",
        )(taps, gain_row, bias_row, wt, out_mixer)
        p, std, inv = call(
            functools.partial(project_body, w=w),
            [((c3, n), BF16), ((c, n), BF16), ((8, n), F32)],
            3,
            limit=16,
            flops=2 * c3 * c * n,
            moved=8 << 20,
            name="project",
        )(x2, w_row, aff)
        up_in = jnp.where(even, across, inside)
        dn_in = jnp.where(even, inside, across)
        mixed, ph, pay, t = call(
            functools.partial(mix_body, w=w, heads=heads),
            [((c3, n), BF16), ((c3, 4 * w), BF16), ((c, 128), F32), ((c, c), F32)],
            9,
            scratch=[
                pltpu.VMEM((c3, 128), F32),
                pltpu.VMEM((2, c, 256), F32),
            ],
            limit=12,
            flops=8 * c * c * n,
            moved=8 << 20,
            name="mix",
        )(flags, p, up_in, dn_in, dy2, w_row, wot, cols, aff)

        half = c // 2
        mine = jnp.where(core == 0, pay[:half], pay[half:])
        theirs = jnp.where(core == 0, pay[half:], pay[:half])
        mine = mine + swap(theirs, 1, total)
        (mh,) = call(
            functools.partial(edge_body, w=w),
            [((c3, 2 * w), BF16)],
            3,
            limit=8,
            moved=6 << 20,
            name="edge",
        )(p, ph, cols)
        for i, mask in enumerate(bits(total, tile)):
            mine = mine + swap(mine, mask, total)
            if i == 0:
                mine, mh = lax.optimization_barrier((mine, mh))
        other = swap(mine, 1, total)

        each = pl.cdiv(c + 32, 2 * chips) * 2
        size = each * chips
        gp, left, right = call(
            functools.partial(back_body, w=w, heads=heads),
            [((c3, n), BF16), ((size, 384), BF16), ((size, 384), BF16)],
            15,
            hbm_out=(0,),
            scratch=[
                pltpu.VMEM((c, 128), F32),
                pltpu.VMEM((640, 128), F32),
                pltpu.VMEM((c3, 9 * 128), F32),
                pltpu.VMEM((2, c, 256), BF16),
                pltpu.VMEM((c, 256), F32),
                pltpu.VMEM((c3, (rows + 2) * w), BF16),
                pltpu.VMEM((c + 16, n), BF16),
                pltpu.VMEM((size, 640), F32),
                pltpu.VMEM((c3, n), BF16),
                pltpu.SemaphoreType.DMA((3,)),
            ],
            limit=24,
            flops=20 * c * c * n,
            moved=8 << 20,
            name="back",
        )(flags, sharpness.reshape(1, heads), mine, other, mixed, mh, p, ph, dy2, up_in, dn_in, std, t, wot, cols)

        (fm,) = call(
            functools.partial(output_body, w=w),
            [((c, rows, w), BF16)],
            6,
            scratch=[pltpu.VMEM((w // 128, c * rows, 128), F32)],
            limit=10,
            flops=2 * c3 * c * n,
            moved=6 << 20,
            name="output",
        )(gp, wt, std, inv, dy3, aff)
        part = jnp.where(core == 0, left, right)
        away = jnp.where(core == 0, right, left)
        part = (part.astype(F32) + swap(away, 1, total).astype(F32)).astype(BF16)
        got = lax.all_to_all(part.reshape(chips, each, 384), GROUP, 0, 0)
        piece = jnp.sum(got.astype(F32), axis=0, keepdims=True).astype(BF16)
        piece, fm = lax.optimization_barrier((piece, fm))
        part = lax.all_to_all(jnp.broadcast_to(piece, got.shape), GROUP, 0, 0)
        part = part.reshape(size, 384)
        rest = swap(part, 1, total)

        outs = call(
            finish_body,
            [((c, c3), F32), ((3, 3, c3), F32), ((c, c), F32), ((1, heads), F32), ((1, c), F32), ((1, c), F32)],
            6,
            scratch=[pltpu.VMEM((size, 768), F32)],
            limit=16,
            name="finish",
            moved=2 << 20,
        )(flags, part, rest, wt, gain_row, bias_row)
        triple_t, taps_t, outgoing, sharp_row, scaling, offset = outs
        return (
            fm.reshape(x.shape),
            triple_t.T,
            jnp.transpose(taps_t, (2, 0, 1)),
            outgoing,
            sharp_row.reshape(heads),
            scaling.reshape(c),
            offset.reshape(c),
        )

    return jax.shard_map(
        local,
        mesh=mesh,
        in_specs=(P("img", None, strip, None), P("img", None, strip, None)) + (P(),) * 6,
        out_specs=(P("img", None, strip, None),) + (P(),) * 6,
        check_vma=False,
    )
```

```python
import functools

import jax
import jax.numpy as jnp
from jax import lax
from jax.experimental import pallas as pl
from jax.experimental.pallas import tpu as pltpu
from jax.sharding import Mesh
from jax.sharding import PartitionSpec as P

F32 = jnp.float32
BF16 = jnp.bfloat16
NT = (((1,), (1,)), ((), ()))
TN = (((0,), (0,)), ((), ()))
VMEM = pl.BlockSpec(memory_space=pltpu.VMEM)
HBM = pl.BlockSpec(memory_space=pltpu.HBM)


def params(limit_mib):
    return pltpu.CompilerParams(vmem_limit_bytes=limit_mib << 20)


def call(body, outs, n_in, hbm_out=(), scratch=(), limit=32, flops=0, name=None, moved=0):
    return pl.pallas_call(
        body,
        out_shape=tuple(jax.ShapeDtypeStruct(s, d) for s, d in outs),
        in_specs=[VMEM for _ in range(n_in)],
        out_specs=tuple(HBM if i in hbm_out else VMEM for i in range(len(outs))),
        scratch_shapes=list(scratch),
        compiler_params=params(limit),
        cost_estimate=pl.CostEstimate(flops=flops, bytes_accessed=moved, transcendentals=0),
        name=name,
    )


def mm(a, b, dims=None, precision=None):
    dims = dims or (((1,), (0,)), ((), ()))
    return lax.dot_general(a, b, dims, preferred_element_type=F32, precision=precision)


def mm_split(a, b, dims=None):
    high = a.astype(BF16)
    low = (a - high.astype(F32)).astype(BF16)
    return mm(high, b, dims) + mm(low, b, dims)


def iota(shape, axis):
    return lax.broadcasted_iota(jnp.int32, shape, axis)


def to_column(row):
    n = row.shape[1]
    eye = iota((n, n), 0) == iota((n, n), 1)
    return jnp.sum(jnp.where(eye, row, 0.0), axis=1, keepdims=True)


def halves(v):
    return [v[:, i : i + 128] for i in range(0, v.shape[1], 128)]


def joined(parts):
    return jnp.concatenate(parts, axis=1)


def shift_right(parts):
    first = iota(parts[0].shape, 1) == 0
    moved = [pltpu.roll(p, 1, 1) for p in parts]
    before = [jnp.zeros_like(parts[0])] + moved[:-1]
    return [jnp.where(first, b, m) for b, m in zip(before, moved)]


def shift_left(parts):
    last = iota(parts[0].shape, 1) == 127
    moved = [pltpu.roll(p, 127, 1) for p in parts]
    after = moved[1:] + [jnp.zeros_like(parts[0])]
    return [jnp.where(last, a, m) for a, m in zip(after, moved)]


def combine(k, window, order):
    count = range(len(window[0]))
    return [
        [sum(k[3 * a + b] * window[order[a]][i] for a in range(3)) for i in count]
        for b in range(3)
    ]


def each_group(total, body, batch=6):
    def trip(g, carry):
        for j in range(batch):
            body(pl.ds(pl.multiple_of((g * batch + j) * 16, 16), 16))
        return carry

    lax.fori_loop(0, total // (16 * batch), trip, 0)


def spread_body(flags, x_ref, dy_ref, x2_ref, dy2_ref, up_ref, dn_ref, s):
    c, rows, w = x_ref.shape
    for j, (src, dst, k, off) in enumerate(((x_ref, x2_ref, 2, 0), (dy_ref, dy2_ref, 1, 2))):
        for q in range(w // 128):
            block = src[:, :, q * 128 : (q + 1) * 128]
            s[j, q] = block.astype(F32).reshape(c * rows, 128)
        for h in range(rows):
            v = [s[j, q, pl.ds(h, c, stride=rows), :] for q in range(w // 128)]
            v = jnp.concatenate(v, axis=1).astype(BF16)
            dst[:, h * w : (h + 1) * w] = v
            if h < k:
                dn_ref[:, (off + h) * w : (off + h + 1) * w] = v
            if h >= rows - k:
                u = off + h - rows + k
                up_ref[:, u * w : (u + 1) * w] = v


def columns_body(taps_ref, gain_ref, bias_ref, wt_ref, wo_ref, cols_ref, affine_ref, w_ref, wot_ref, wide):
    n = taps_ref.shape[2]
    c = gain_ref.shape[1]
    wide[...] = jnp.zeros_like(wide)
    for a in range(3):
        for b in range(3):
            wide[3 * a + b : 3 * a + b + 1, 0:n] = taps_ref[a, b : b + 1, :]
    w_ref[...] = wt_ref[...].astype(F32).T.astype(BF16)
    wot_ref[...] = wo_ref[...].astype(F32).T.astype(BF16)
    wide[9:10, 0:c] = gain_ref[...]
    wide[10:11, 0:c] = bias_ref[...]
    for g in range(0, 640, 128):
        flat = wide[:, g : g + 128].T
        m = min(128, n - g)
        for t in range(9):
            cols_ref[t, g : g + m, :] = jnp.broadcast_to(flat[0:m, t : t + 1], (m, 128))
        if g < c:
            m = min(128, c - g)
            for t in range(2):
                affine_ref[t, g : g + m, :] = jnp.broadcast_to(flat[0:m, 9 + t : 10 + t], (m, 128))


def affine(affine_ref, w):
    return [jnp.concatenate([affine_ref[i]] * (w // 128), axis=1) for i in range(2)]


def normalise(x, gain, bias):
    average = jnp.mean(x, axis=0, keepdims=True)
    centered = x - average
    inverse = lax.rsqrt(jnp.mean(centered * centered, axis=0, keepdims=True) + 1e-05)
    standard = centered * inverse
    return standard, inverse, (standard * gain + bias).astype(BF16)


def project_body(x2_ref, w_ref, affine_ref, p_ref, std_ref, inv_ref, *, w):
    gain, bias = affine(affine_ref, w)
    for h in range(x2_ref.shape[1] // w):
        at = slice(h * w, (h + 1) * w)
        standard, inverse, normed = normalise(x2_ref[:, at].astype(F32), gain, bias)
        std_ref[:, at] = standard.astype(BF16)
        inv_ref[:, at] = jnp.broadcast_to(inverse, (8, w))
        p_ref[:, at] = mm(w_ref[...], normed).astype(BF16)


def mix_rows(first, last, row, cols_ref, ch, put):
    k = [cols_ref[t, ch, :] for t in range(9)]
    window = [row(first - 1), row(first), None]
    for r in range(first, last):
        window[2] = row(r + 1)
        u = combine(k, window, (0, 1, 2))
        put(r, [x + y + z for x, y, z in zip(u[1], shift_right(u[0]), shift_left(u[2]))])
        window = [window[1], window[2], None]


def row_reader(p_ref, ph_ref, ch, w):
    rows = p_ref.shape[1] // w

    def row(r):
        if r < 0:
            return ph_ref[ch, (r + 2) * w : (r + 3) * w]
        if r >= rows:
            return ph_ref[ch, (r - rows + 2) * w : (r - rows + 3) * w]
        return p_ref[ch, r * w : (r + 1) * w]

    return row


def wide_reader(p_ref, ph_ref, ch, w):
    row = row_reader(p_ref, ph_ref, ch, w)
    return lambda r: [v.astype(F32) for v in halves(row(r))]


def store_rows(out_ref, total, ch, w):
    def put(at, out):
        out = joined(out).astype(BF16)
        out_ref[ch, at * w : (at + 1) * w] = out
        for v in halves(out):
            v = v.astype(F32)
            total[:] = [total[0] + v * v] if total else [v * v]

    return put


def inner_body(p_ref, cols_ref, mi_ref, sq_ref, *, w):
    rows = p_ref.shape[1] // w

    def group(ch):
        total = []
        put = store_rows(mi_ref, total, ch, w)
        row = wide_reader(p_ref, None, ch, w)
        mix_rows(1, rows - 1, row, cols_ref, ch, lambda r, out: put(r - 1, out))
        sq_ref[ch, :] = total[0]

    each_group(p_ref.shape[0], group)


def mix_body(
    flags, p_ref, up_ref, dn_ref, dy2_ref, w_ref, wot_ref, cols_ref, affine_ref, mi_ref, sqi_ref,
    mo_ref, ph_ref, pay_ref, t_ref, sq, gs, *, w, heads,
):
    c3 = p_ref.shape[0]
    c = c3 // 3
    hs = c // heads
    rows = p_ref.shape[1] // w
    gain, bias = affine(affine_ref, w)
    keep_up = flags[0:1, 0:1]
    keep_dn = flags[1:2, 0:1]
    for src, keep, base in ((up_ref, keep_up, 0), (dn_ref, keep_dn, 2)):
        for h in range(2):
            normed = normalise(src[:, h * w : (h + 1) * w].astype(F32), gain, bias)[2]
            at = slice((base + h) * w, (base + h + 1) * w)
            ph_ref[:, at] = (mm(w_ref[...], normed) * keep).astype(BF16)

    def group(ch):
        total = [sqi_ref[ch, :]]
        put = store_rows(mo_ref, total, ch, w)
        row = wide_reader(p_ref, ph_ref, ch, w)
        for i, r in enumerate((0, rows - 1)):
            mix_rows(r, r + 1, row, cols_ref, ch, lambda _, out, i=i: put(i, out))
        sq[ch, :] = total[0]

    each_group(c3, group)

    gram = mm(mi_ref[0:c, :], mi_ref[c : 2 * c, :], NT)
    gs[0, :, 0:c] = gram + mm(mo_ref[0:c, :], mo_ref[c : 2 * c, :], NT)
    last = (rows - 1) * w
    t = mm(dy2_ref[:, w:last], mi_ref[2 * c : 3 * c, :], NT)
    t = t + mm(dy2_ref[:, 0:w], mo_ref[2 * c : 3 * c, 0:w], NT)
    t = t + mm(dy2_ref[:, last:], mo_ref[2 * c : 3 * c, w:], NT)
    t_ref[...] = t
    high = t.astype(BF16)
    low = (t - high.astype(F32)).astype(BF16)
    gs[1, :, 0:c] = mm(wot_ref[...], high) + mm(wot_ref[...], low)
    lane = iota((hs, 128), 1)
    for h in range(heads):
        at = slice(h * hs, (h + 1) * hs)
        gram = pltpu.roll(gs[0, at, :], (256 - hs * h) % 256, 1)[:, 0:128]
        grad = pltpu.roll(gs[1, at, :], (256 + hs - hs * h) % 256, 1)[:, 0:128]
        query_sq = jnp.sum(sq[at, :], axis=1, keepdims=True)
        key_sq = jnp.sum(sq[c + h * hs : c + (h + 1) * hs, :], axis=1, keepdims=True)
        rest = jnp.where(lane == 2 * hs, query_sq, key_sq)
        pay_ref[at, :] = jnp.where(lane < hs, gram, jnp.where(lane < 2 * hs, grad, rest))


def edge_body(p_ref, ph_ref, cols_ref, wot_ref, dy2_ref, up_ref, dn_ref, mh_ref, ga_ref, *, w):
    rows = p_ref.shape[1] // w
    wot = wot_ref[...]
    ga_ref[:, 0:w] = mm(wot, up_ref[:, 2 * w : 3 * w]).astype(BF16)
    for r in range(rows):
        ga_ref[:, (r + 1) * w : (r + 2) * w] = mm(wot, dy2_ref[:, r * w : (r + 1) * w]).astype(BF16)
    ga_ref[:, (rows + 1) * w :] = mm(wot, dn_ref[:, 2 * w : 3 * w]).astype(BF16)

    def group(ch):
        row = wide_reader(p_ref, ph_ref, ch, w)
        for i, r in enumerate((-1, rows)):
            def put(_, out):
                mh_ref[ch, i * w : (i + 1) * w] = joined(out).astype(BF16)

            mix_rows(r, r + 1, row, cols_ref, ch, put)

    each_group(p_ref.shape[0], group)


def back_body(
    flags, sharp, mine_ref, other_ref, mi_ref, mo_ref, mh_ref, ga_ref, p_ref, ph_ref,
    std_ref, t_ref, cols_ref,
    gp_hbm, left_ref, right_ref, pay, coef, sums, mats, vecs, gm, aug, grads, gp_ref, sem, *, w, heads,
):
    c = p_ref.shape[0] // 3
    hs = c // heads
    rows = p_ref.shape[1] // w
    mine = mine_ref[...]
    other = other_ref[...]
    first_core = jnp.broadcast_to(flags[3:4, :], mine.shape) < 0.5
    pay[0 : c // 2, :] = jnp.where(first_core, mine, other)
    pay[c // 2 : c, :] = jnp.where(first_core, other, mine)
    lane = iota((hs, 128), 1)
    valid = lane < hs
    eye = lane == iota((hs, 128), 0)
    pad = jnp.zeros((hs, 128), F32)
    sharp_row = jnp.zeros((1, 128), F32)
    for h in range(heads):
        at = slice(h * hs, (h + 1) * hs)
        block = pay[at, :]
        gram = jnp.where(valid, block, 0.0)
        grad = jnp.where(valid, pltpu.roll(block, 128 - hs, 1), 0.0)
        query_sq = block[:, 2 * hs : 2 * hs + 1] + 1e-06
        key_sq = (
            jnp.sum(jnp.where(eye, block[:, 2 * hs + 1 : 2 * hs + 2], 0.0), axis=0, keepdims=True)
            + 1e-06
        )
        length = jnp.sqrt(query_sq) * jnp.sqrt(key_sq)
        cosine = gram / length
        weights = jnp.where(valid, jnp.exp(cosine * sharp[0:1, h : h + 1]), 0.0)
        attention = weights / jnp.sum(weights, axis=1, keepdims=True)
        scores = attention * (grad - jnp.sum(attention * grad, axis=1, keepdims=True))
        terms = scores * cosine
        sharp_h = jnp.sum(jnp.sum(terms, axis=1, keepdims=True), axis=0, keepdims=True)
        sharp_row = jnp.where(iota((1, 128), 1) == h, sharp_h, sharp_row)
        grad_cos = scores * sharp[0:1, h : h + 1]
        terms = grad_cos * cosine
        alpha = jnp.sum(terms, axis=1, keepdims=True) / query_sq
        beta = jnp.sum(terms, axis=0, keepdims=True) / key_sq
        beta = jnp.sum(jnp.where(eye, beta, 0.0), axis=1, keepdims=True)
        vecs[at, 0:128] = jnp.broadcast_to(alpha, (hs, 128))
        vecs[at, 128:256] = jnp.broadcast_to(beta, (hs, 128))
        for i, m in enumerate((grad_cos / length, attention)):
            placed = pltpu.roll(jnp.concatenate([m, pad], axis=1), hs * h, 1)
            mats[i, at, :] = placed.astype(BF16)

    grad_gram = mats[0, :, 0:c]
    grad_gram_t = grad_gram.astype(F32).T.astype(BF16)
    attention_b = mats[1, :, 0:c]
    attention_t = attention_b.astype(F32).T.astype(BF16)
    outgoing = mm_split(t_ref[...], attention_b, NT)
    alpha = jnp.concatenate([vecs[:, 0:128]] * (w // 128), axis=1)
    beta = jnp.concatenate([vecs[:, 128:256]] * (w // 128), axis=1)
    for r in range(rows + 2):
        at = slice(r * w, (r + 1) * w)
        if r in (0, rows + 1):
            src, own = (mh_ref, 0 if r == 0 else 1)
        elif r in (1, rows):
            src, own = (mo_ref, 0 if r == 1 else 1)
        else:
            src, own = (mi_ref, r - 2)
        own = slice(own * w, (own + 1) * w)
        query = src[0:c, own]
        key = src[c : 2 * c, own]
        grad_attended = ga_ref[:, at]
        parts = (
            mm(grad_gram, key) - query.astype(F32) * alpha,
            mm(grad_gram_t, query) - key.astype(F32) * beta,
            mm(attention_t, grad_attended),
        )
        for i, part in enumerate(parts):
            if r == 0:
                part = part * flags[0:1, 0:1]
            if r == rows + 1:
                part = part * flags[1:2, 0:1]
            gm[i * c : (i + 1) * c, at] = part.astype(BF16)

    def input_grad(ch):
        k = [cols_ref[t, ch, :] for t in range(9)]

        def row(r):
            return [v.astype(F32) for v in halves(gm[ch, r * w : (r + 1) * w])]

        window = [None, row(0), row(1)]
        for r in range(rows):
            window = [window[1], window[2], row(r + 2)]
            u = combine(k, window, (2, 1, 0))
            out = [x + y + z for x, y, z in zip(u[1], shift_left(u[0]), shift_right(u[2]))]
            gp_ref[ch, r * w : (r + 1) * w] = joined(out).astype(BF16)

    each_group(3 * c, input_grad)
    copies = []
    for i in range(3):
        at = pl.ds(i * c, c)
        copies.append(pltpu.make_async_copy(gp_ref.at[at], gp_hbm.at[at], sem.at[i]))
        copies[-1].start()

    def stencil(ch):
        row = wide_reader(p_ref, ph_ref, ch, w)
        acc = [None] * 9
        window = [None, row(-1), row(0)]
        for r in range(rows):
            window = [window[1], window[2], row(r + 1)]
            v = [x.astype(F32) for x in halves(gm[ch, (r + 1) * w : (r + 2) * w])]
            moved = (shift_left(v), v, shift_right(v))
            for t in range(9):
                for x, y in zip(moved[t % 3], window[t // 3]):
                    acc[t] = x * y if acc[t] is None else acc[t] + x * y
        for t in range(9):
            sums[ch, t * 128 : (t + 1) * 128] = acc[t]

    each_group(3 * c, stencil)
    place = iota((9 * 128, 128), 0) // 128 == iota((9 * 128, 128), 1)
    place = jnp.where(place, 1.0, 0.0).astype(BF16)
    for g in range(0, 3 * c, 64):
        block = sums[g : g + 64, :]
        coef[g : g + 64, :] = mm_split(block, place)

    aug[0:c, :] = std_ref[...]
    aug[c : c + 16, :] = jnp.where(iota((16, rows * w), 0) == 0, 1.0, 0.0).astype(BF16)
    c3 = 3 * c
    grads[...] = jnp.zeros_like(grads)
    grads[0 : c + 16, 0:c3] = mm(aug[...], gp_ref[...], NT)
    grads[c + 16 : c + 32, :] = coef[...].T[0:16, :]
    grads[c + 1 : c + 2, 0:128] = sharp_row * flags[2:3, :]
    out_pad = jnp.concatenate([outgoing, jnp.zeros((c, 256 - c), F32)], axis=1)
    half = c3 % 128
    tail = grads[0:c, c3 - half : c3 - half + 128]
    moved = pltpu.roll(out_pad[:, 128:256], half, 1)
    grads[0:c, c3 - half : c3 - half + 128] = jnp.where(iota((c, 128), 1) < half, tail, moved)
    left_ref[...] = grads[:, 0:384].astype(BF16)
    right_ref[:, 0:256] = grads[:, 384:640].astype(BF16)
    right_ref[0:c, 256:384] = out_pad[:, 0:128].astype(BF16)
    right_ref[c:, 256:384] = jnp.zeros((grads.shape[0] - c, 128), BF16)
    for copy in copies:
        copy.wait()


def output_body(gp_ref, wt_ref, std_ref, inv_ref, dy_ref, affine_ref, out_ref, s, *, w):
    c, rows, _ = out_ref.shape
    gain = affine(affine_ref, w)[0]
    for h in range(rows):
        at = slice(h * w, (h + 1) * w)
        scaled = mm(wt_ref[...], gp_ref[:, at]) * gain
        standard = std_ref[:, at].astype(F32)
        first = jnp.mean(scaled, axis=0, keepdims=True)
        second = jnp.mean(scaled * standard, axis=0, keepdims=True)
        v = (scaled - first - standard * second) * inv_ref[0:1, at]
        for i in range(w // 128):
            s[i, pl.ds(h, c, stride=rows), :] = v[:, i * 128 : (i + 1) * 128]
    for i in range(w // 128):
        at = slice(i * 128, (i + 1) * 128)
        v = dy_ref[:, :, at].astype(F32) + s[i, :, :].reshape(c, rows, 128)
        out_ref[:, :, at] = v.astype(BF16)


def finish_body(
    flags, mine_ref, other_ref, wt_ref, gain_ref, bias_ref,
    triple_ref, taps_ref, outgoing_ref, sharp_ref, scaling_ref, offset_ref, full,
):
    c, c3 = wt_ref.shape
    mine = mine_ref[...].astype(F32)
    other = other_ref[...].astype(F32)
    first_core = jnp.broadcast_to(flags[3:4, 0:1], mine.shape) < 0.5
    full[:, 0:384] = jnp.where(first_core, mine, other)
    full[:, 384:768] = jnp.where(first_core, other, mine)
    m = full[0:c, 0:c3]
    s = full[c : c + 1, 0:c3]
    gain = to_column(gain_ref[...])
    bias = to_column(bias_ref[...])
    wt = wt_ref[...].astype(F32)
    triple_ref[...] = m * gain + bias * s
    eye = iota((c, c), 0) == iota((c, c), 1)
    scaling = jnp.sum(wt * m, axis=1, keepdims=True)
    offset = jnp.sum(wt * s, axis=1, keepdims=True)
    scaling_ref[...] = jnp.sum(jnp.where(eye, scaling, 0.0), axis=0, keepdims=True)
    offset_ref[...] = jnp.sum(jnp.where(eye, offset, 0.0), axis=0, keepdims=True)
    for a in range(3):
        taps_ref[a, :, :] = full[c + 16 + 3 * a : c + 19 + 3 * a, 0:c3]
    half = c3 % 128
    outgoing_ref[:, 0:128] = full[0:c, 640:768]
    tail = pltpu.roll(full[0:c, 512:640], 128 - half, 1)
    outgoing_ref[:, 128:c] = tail[:, 0 : c - 128]
    sharp_ref[...] = full[c + 1 : c + 2, 0 : sharp_ref.shape[1]]


GROUP = ("img", "chip")
ALL = ("img", "chip", "core")


def swap(v, mask, count):
    return lax.ppermute(v, ALL, [(i, i ^ mask) for i in range(count)])


def bits(total, tile):
    if total == 256 and tile == 32:
        return (2, 6, 8, 16)
    return tuple(1 << i for i in range(1, 20) if 1 << i < tile)


def solution(mesh):
    img, tile = (mesh.shape["img"], mesh.shape["tile"])
    total = img * tile
    chips = total // 2
    mesh = Mesh(mesh.devices.reshape(img, tile // 2, 2), ALL)
    strip = ("chip", "core")

    def local(x, dy, triple, stencil, out_mixer, sharpness, gain, bias):
        _, c, rows, w = x.shape
        heads = sharpness.shape[0]
        c3 = 3 * c
        n = rows * w
        ext = n + 2 * w
        core = lax.axis_index("core")
        place = lax.axis_index("chip") * 2 + core
        flags = jnp.stack([place != 0, place != tile - 1, place == 0, core == 1]).astype(F32)
        flags = jnp.broadcast_to(jnp.pad(flags, (0, 4))[:, None], (8, 128))
        x3 = x.reshape(c, rows, w)
        dy3 = dy.reshape(c, rows, w)
        taps = jnp.transpose(stencil, (1, 2, 0))
        wt = triple.T
        gain_row = gain.reshape(1, c)
        bias_row = bias.reshape(1, c)

        x2, dy2, up, dn = call(
            spread_body,
            [((c, n), BF16), ((c, n), BF16), ((c, 3 * w), BF16), ((c, 3 * w), BF16)],
            3,
            scratch=[pltpu.VMEM((2, w // 128, c * rows, 128), F32)],
            limit=8,
            name="spread",
            moved=4 << 20,
        )(flags, x3, dy3)
        even = core == 0
        inside = lax.ppermute(jnp.where(even, up, dn), strip, [(i, i ^ 1) for i in range(tile)])
        pairs = [(i, i + 1) for i in range(1, tile - 1, 2)]
        across = jnp.where(even, dn, up)
        across = lax.ppermute(across, strip, pairs + [(j, i) for i, j in pairs])
        cols, aff, w_row, wot = call(
            columns_body,
            [((9, c3, 128), F32), ((2, c, 128), F32), ((c3, c), BF16), ((c, c), BF16)],
            5,
            scratch=[pltpu.VMEM((128, 640), F32)],
            limit=16,
            moved=4 << 20,
            name="columns",
        )(taps, gain_row, bias_row, wt, out_mixer)
        p, std, inv = call(
            functools.partial(project_body, w=w),
            [((c3, n), BF16), ((c, n), BF16), ((8, n), F32)],
            3,
            limit=16,
            flops=2 * c3 * c * n,
            moved=8 << 20,
            name="project",
        )(x2, w_row, aff)
        mi, sqi = call(
            functools.partial(inner_body, w=w),
            [((c3, n - 2 * w), BF16), ((c3, 128), F32)],
            2,
            limit=8,
            flops=400 * c3 * n,
            moved=8 << 20,
            name="inner",
        )(p, cols)
        up_in = jnp.where(even, across, inside)
        dn_in = jnp.where(even, inside, across)
        mo, ph, pay, t = call(
            functools.partial(mix_body, w=w, heads=heads),
            [((c3, 2 * w), BF16), ((c3, 4 * w), BF16), ((c, 128), F32), ((c, c), F32)],
            11,
            scratch=[
                pltpu.VMEM((c3, 128), F32),
                pltpu.VMEM((2, c, 256), F32),
            ],
            limit=12,
            flops=8 * c * c * n,
            moved=8 << 20,
            name="mix",
        )(flags, p, up_in, dn_in, dy2, w_row, wot, cols, aff, mi, sqi)

        half = c // 2
        mine = jnp.where(core == 0, pay[:half], pay[half:])
        theirs = jnp.where(core == 0, pay[half:], pay[:half])
        mine = mine + swap(theirs, 1, total)
        mh, ga = call(
            functools.partial(edge_body, w=w),
            [((c3, 2 * w), BF16), ((c, ext), BF16)],
            7,
            limit=8,
            moved=6 << 20,
            name="edge",
        )(p, ph, cols, wot, dy2, up_in, dn_in)
        for i, mask in enumerate(bits(total, tile)):
            mine = mine + swap(mine, mask, total)
            if i == 0:
                mine, mh, ga = lax.optimization_barrier((mine, mh, ga))
        other = swap(mine, 1, total)

        each = pl.cdiv(c + 32, 2 * chips) * 2
        size = each * chips
        gp, left, right = call(
            functools.partial(back_body, w=w, heads=heads),
            [((c3, n), BF16), ((size, 384), BF16), ((size, 384), BF16)],
            13,
            hbm_out=(0,),
            scratch=[
                pltpu.VMEM((c, 128), F32),
                pltpu.VMEM((640, 128), F32),
                pltpu.VMEM((c3, 9 * 128), F32),
                pltpu.VMEM((2, c, 256), BF16),
                pltpu.VMEM((c, 256), F32),
                pltpu.VMEM((c3, (rows + 2) * w), BF16),
                pltpu.VMEM((c + 16, n), BF16),
                pltpu.VMEM((size, 640), F32),
                pltpu.VMEM((c3, n), BF16),
                pltpu.SemaphoreType.DMA((3,)),
            ],
            limit=24,
            flops=20 * c * c * n,
            moved=8 << 20,
            name="back",
        )(flags, sharpness.reshape(1, heads), mine, other, mi, mo, mh, ga, p, ph, std, t, cols)

        (fm,) = call(
            functools.partial(output_body, w=w),
            [((c, rows, w), BF16)],
            6,
            scratch=[pltpu.VMEM((w // 128, c * rows, 128), F32)],
            limit=10,
            flops=2 * c3 * c * n,
            moved=6 << 20,
            name="output",
        )(gp, wt, std, inv, dy3, aff)
        part = jnp.where(core == 0, left, right)
        away = jnp.where(core == 0, right, left)
        part = (part.astype(F32) + swap(away, 1, total).astype(F32)).astype(BF16)
        got = lax.all_to_all(part.reshape(chips, each, 384), GROUP, 0, 0)
        piece = jnp.sum(got.astype(F32), axis=0, keepdims=True).astype(BF16)
        piece, fm = lax.optimization_barrier((piece, fm))
        part = lax.all_to_all(jnp.broadcast_to(piece, got.shape), GROUP, 0, 0)
        part = part.reshape(size, 384)
        rest = swap(part, 1, total)

        outs = call(
            finish_body,
            [((c, c3), F32), ((3, 3, c3), F32), ((c, c), F32), ((1, heads), F32), ((1, c), F32), ((1, c), F32)],
            6,
            scratch=[pltpu.VMEM((size, 768), F32)],
            limit=16,
            name="finish",
            moved=2 << 20,
        )(flags, part, rest, wt, gain_row, bias_row)
        triple_t, taps_t, outgoing, sharp_row, scaling, offset = outs
        return (
            fm.reshape(x.shape),
            triple_t.T,
            jnp.transpose(taps_t, (2, 0, 1)),
            outgoing,
            sharp_row.reshape(heads),
            scaling.reshape(c),
            offset.reshape(c),
        )

    return jax.shard_map(
        local,
        mesh=mesh,
        in_specs=(P("img", None, strip, None), P("img", None, strip, None)) + (P(),) * 6,
        out_specs=(P("img", None, strip, None),) + (P(),) * 6,
        check_vma=False,
    )
```
